32 devices in a mesh: region: 8 (over z, x), dp: 4 (over y, core).
Axes of the slice: x: 2, y: 2, z: 4, core: 2. Of those that a mesh axis runs over, the one named last changes fastest.
Arguments:
- features: bfloat16 [4, 16384, 192], P('dp', 'region')
- weight: bfloat16 [27, 192, 192], replicated, may hold values from -0.078125 to 0.078125
- norm_gain: float32 [192], replicated, may hold values from 0.5 to 2
- norm_shift: float32 [192], replicated, may hold values from -1 to 1
- cotangent: bfloat16 [4, 16384, 192], P('dp', 'region'), may hold values from -6 to 6
- counts: int32 [4, 8], P('dp', 'region'), may hold values from 1024 to 2048, as said below
- in_rows: int32 [4, 8, 27, 1024], P('dp', 'region'), may hold values from 0 to 2047, as said below
- out_slots: int32 [4, 8, 27, 1024], P('dp', 'region'), may hold values from 0 to 3072, as said below
- land_rows: int32 [4, 8, 8, 128], P('dp', 'region'), may hold values from 0 to 2047, as said below
Outputs:
- activated: bfloat16 [4, 16384, 192], P('dp', 'region')
- input_grad: bfloat16 [4, 16384, 192], P('dp', 'region')
- weight_grad: float32 [27, 192, 192], replicated
- gain_grad: float32 [192], replicated
- shift_grad: float32 [192], replicated
The draws below stay inside these ranges and needn't reach their ends.
Inputs may be any that keep to these rules, and one draw needn't show every extreme that they name: `counts`: A multiple of 128, at least 1024; in every scan some region holds exactly 2048 rows. `in_rows`: pair p of an offset is live when p < counts // 2 of its region, and then names a row below the region's count; other pairs name row 0. `out_slots`: A live pair targets a local row below the region's count, or slot p of direction j as 2048 + j * 128 + p, only where the region of direction j exists on the grid of 1 row by 8 columns; other pairs target 2048 + 8 * 128. `land_rows`: below the count of the receiving region.
All inputs are finite; a program needn't handle non-finite values.
Results may differ from the reference program's by a relative error of at most 0.0075.
Values may be sent and summed in bfloat16 or wider, within the bound.
No kernel may reach another device: no remote copies, remote signals or barrier semaphores. Data moves between devices by JAX's collectives and lax.ppermute only.
A program may use at most 64 MiB of HBM per device.

```python
import math
import jax
import jax.numpy as jnp
from jax import lax

C = 192
OFFSETS = 27
GRID_W = 8
BLOCK = 128
ROWS_DEV = 2048
PAIRS = 1024
CAP = 128
SCANS = 4
REGIONS = 8
VOXELS = 16384


DIRECTIONS = ((-1, -1), (-1, 0), (-1, 1), (0, -1), (0, 1), (1, -1), (1, 0), (1, 1))


def shared_maps(key):
    seeds = [jax.random.fold_in(key, 7001 + number) for number in range(8)]
    blocks = ROWS_DEV // BLOCK
    block_count = jax.random.randint(seeds[0], (SCANS, REGIONS), blocks // 2, blocks + 1)
    full_region = jax.random.randint(seeds[1], (SCANS, 1), 0, REGIONS)
    block_count = jnp.where(jnp.arange(REGIONS)[None, :] == full_region, blocks, block_count)
    counts = (block_count * BLOCK).astype(jnp.int32)
    bound = counts[:, :, None, None]
    shape = (SCANS, REGIONS, OFFSETS, PAIRS)
    pair_ids = jnp.arange(PAIRS).astype(jnp.int32)[None, None, None, :]
    live_pairs = pair_ids < bound // 2
    sources = jax.random.randint(seeds[2], shape, 0, bound)
    sources = jnp.where(pair_ids == 0, bound - 1, sources)
    local_target = jax.random.randint(seeds[3], shape, 0, bound)
    boundary = jax.random.randint(seeds[4], shape, 0, 4) == 0
    slot_dir = jax.random.randint(seeds[5], shape, 0, 8)
    slot_pos = jax.random.randint(seeds[6], shape, 0, CAP)
    region_ids = jnp.arange(REGIONS).astype(jnp.int32)[None, :, None, None]
    grid_row = region_ids // GRID_W
    grid_col = region_ids % GRID_W
    row_table = jnp.array([offset_pair[0] for offset_pair in DIRECTIONS], jnp.int32)
    col_table = jnp.array([offset_pair[1] for offset_pair in DIRECTIONS], jnp.int32)
    neighbour_row = grid_row + row_table[slot_dir]
    neighbour_col = grid_col + col_table[slot_dir]
    valid = (neighbour_row >= 0) & (neighbour_row < REGIONS // GRID_W) & (neighbour_col >= 0) & (neighbour_col < GRID_W)
    targets = jnp.where(boundary & valid, ROWS_DEV + slot_dir * CAP + slot_pos, local_target)
    discard = ROWS_DEV + 8 * CAP
    in_rows = jnp.where(live_pairs, sources, 0).astype(jnp.int32)
    out_slots = jnp.where(live_pairs, targets, discard).astype(jnp.int32)
    land_bound = counts[:, :, None, None]
    land_rows = jax.random.randint(seeds[7], (SCANS, REGIONS, 8, CAP), 0, land_bound)
    first_slot = (jnp.arange(8)[:, None] == 0) & (jnp.arange(CAP)[None, :] == 0)
    land_rows = jnp.where(first_slot[None, None], land_bound - 1, land_rows).astype(jnp.int32)
    return (counts, in_rows, out_slots, land_rows)


def draw_counts(key, part):
    return shared_maps(key)[0]


def draw_in_rows(key, part):
    return shared_maps(key)[1]


def draw_out_slots(key, part):
    return shared_maps(key)[2]


def draw_land_rows(key, part):
    return shared_maps(key)[3]


def draw_features(key, part):
    seeds = [jax.random.fold_in(key, 9101 + number) for number in range(3)]
    shape = (SCANS, VOXELS, C)
    base = jax.random.normal(seeds[0], shape, jnp.float32)
    row_log = jax.random.uniform(seeds[1], (SCANS, VOXELS, 1), jnp.float32, 0.0, 2.3026)
    col_log = jax.random.uniform(seeds[2], (1, 1, C), jnp.float32, 0.0, 2.3026)
    region = (jnp.arange(VOXELS) // ROWS_DEV).astype(jnp.float32)
    rising = (1.0 + 2.0 * region / max(REGIONS - 1, 1))[None, :, None]
    return (base * jnp.exp(row_log - 1.15) * jnp.exp(col_log - 1.15) * rising).astype(jnp.bfloat16)


def levels(own_key, extent, pieces, least, top_value):
    level = 1.0
    for dim, shards_of in pieces:
        heights = jax.random.uniform(jax.random.fold_in(jax.random.fold_in(own_key, 6), dim), (shards_of,), jnp.float32, least / len(pieces), top_value / len(pieces))
        level = level * jnp.repeat(jnp.exp(heights), extent[dim] // shards_of).reshape((-1,) + (1,) * (len(extent) - 1 - dim))
    return level


def centred(own_key, shape, width, reach, shards=(), kind=jnp.bfloat16):
    values = width * jax.random.normal(own_key, shape, jnp.float32)
    if shards:
        values = values * levels(own_key, shape, shards, -0.22, 0.18)
    return jnp.clip(values, -reach, reach).astype(kind)


def setup_inputs(seed: int = 0) -> dict:
    key_list = jax.random.split(jax.random.key(seed), 10)
    return {
        "features": draw_features(jax.random.fold_in(key_list[9], 71), 0),
        "weight": centred(key_list[1], (OFFSETS, C, C), (OFFSETS * C) ** -0.5, 0.078125),
        "norm_gain": jnp.clip(jnp.exp(jax.random.uniform(key_list[2], (C,), jnp.float32, math.log(0.5), math.log(2.0))), 0.5, 2.0),
        "norm_shift": jnp.clip(jax.random.uniform(key_list[3], (C,), jnp.float32, -1.0, 1.0), -1.0, 1.0),
        "cotangent": centred(key_list[4], (SCANS, VOXELS, C), 1.0, 6.0, ((0, 4), (1, 8))),
        "counts": draw_counts(jax.random.fold_in(key_list[9], 71), 0),
        "in_rows": draw_in_rows(jax.random.fold_in(key_list[9], 71), 0),
        "out_slots": draw_out_slots(jax.random.fold_in(key_list[9], 71), 0),
        "land_rows": draw_land_rows(jax.random.fold_in(key_list[9], 71), 0),
    }


DIRECTIONS = ((-1, -1), (-1, 0), (-1, 1), (0, -1), (0, 1), (1, -1), (1, 0), (1, 1))
EPSILON = 1e-05

def forward_local(voxels, weight, sources, targets, extended):

    def advance(summed, member):
        kernel, from_rows, to_rows = member
        partial_sum = jnp.dot(voxels[from_rows], kernel, preferred_element_type=jnp.float32)
        return (summed.at[to_rows].add(partial_sum), None)
    start = jnp.zeros((extended, voxels.shape[1]), jnp.float32)
    summed, unused = lax.scan(advance, start, (weight, sources, targets))
    return summed

def move_slots(slot_data, direction_sign):
    region_ids = jnp.arange(REGIONS).astype(jnp.int32)
    moved = []
    for slot_dir, offset_pair in enumerate(DIRECTIONS):
        offset = direction_sign * (offset_pair[0] * GRID_W + offset_pair[1])
        source = region_ids - offset
        inside = (source >= 0) & (source < REGIONS)
        taken = jnp.take(slot_data[:, :, slot_dir], jnp.clip(source, 0, REGIONS - 1).astype(jnp.int32), axis=1)
        moved.append(jnp.where(inside[None, :, None, None], taken, jnp.zeros_like(taken)))
    return jnp.stack(moved, axis=2)

def reference(features, weight, norm_gain, norm_shift, cotangent, counts, in_rows, out_slots, land_rows):
    devices = SCANS * REGIONS
    extended = ROWS_DEV + 8 * CAP + 1
    voxels = features.reshape(devices, ROWS_DEV, C)
    sources = in_rows.reshape(devices, OFFSETS, PAIRS)
    targets = out_slots.reshape(devices, OFFSETS, PAIRS)
    places = land_rows.reshape(devices, 8 * CAP)
    summed = lax.map(lambda packed: forward_local(packed[0], weight, packed[1], packed[2], extended), (voxels, sources, targets))
    outgoing = summed[:, ROWS_DEV:ROWS_DEV + 8 * CAP].reshape(SCANS, REGIONS, 8, CAP, C)
    arrived = move_slots(outgoing, 1).reshape(devices, 8 * CAP, C)
    preact = jax.vmap(lambda initial, spots_in, arrivals: initial.at[spots_in].add(arrivals))(summed[:, :ROWS_DEV], places, arrived)
    alive = (jnp.arange(ROWS_DEV)[None, :] < counts.reshape(devices, 1)).astype(jnp.float32)[:, :, None]
    count_total = jnp.sum(counts).astype(jnp.float32)
    average = lax.optimization_barrier(jnp.sum(preact * alive, axis=(0, 1))) / count_total
    centered = (preact - average) * alive
    variance = lax.optimization_barrier(jnp.sum(centered * centered, axis=(0, 1))) / count_total
    inverse = lax.rsqrt(variance + EPSILON)
    normed = (preact - average) * inverse
    shifted = norm_gain * normed + norm_shift
    sigma = jax.nn.sigmoid(shifted)
    slope = sigma * (1.0 + shifted * (1.0 - sigma)) * alive
    activated = (shifted * sigma * alive).astype(jnp.bfloat16)
    upstream = cotangent.reshape(devices, ROWS_DEV, C).astype(jnp.float32) * slope
    gain_grad = lax.optimization_barrier(jnp.sum(upstream * normed, axis=(0, 1)))
    shift_grad = lax.optimization_barrier(jnp.sum(upstream, axis=(0, 1)))
    pre_grad = (norm_gain * inverse * (upstream - shift_grad / count_total - normed * gain_grad / count_total) * alive).astype(jnp.bfloat16)
    picked = jax.vmap(lambda gradient, spots_in: gradient[spots_in])(pre_grad, places).reshape(SCANS, REGIONS, 8, CAP, C)
    returned = move_slots(picked, -1).reshape(devices, 8 * CAP, C)
    padding = jnp.zeros((devices, 1, C), jnp.bfloat16)
    grad_ext = jnp.concatenate([pre_grad, returned, padding], axis=1)

    def backward_device(running, packed):
        voxel_rows, grad_rows, source_rows, target_rows = packed

        def advance(summed_back, member):
            kernel, from_rows, to_rows = member
            gathered = grad_rows[to_rows]
            product = lax.dot_general(gathered, kernel, (((1,), (1,)), ((), ())), preferred_element_type=jnp.float32)
            summed_back = summed_back.at[from_rows].add(product)
            kernel_grad = lax.dot_general(voxel_rows[from_rows], gathered, (((0,), (0,)), ((), ())), preferred_element_type=jnp.float32)
            return (summed_back, kernel_grad)
        start = jnp.zeros((ROWS_DEV, C), jnp.float32)
        summed_back, kernel_grads = lax.scan(advance, start, (weight, source_rows, target_rows))
        return (running + kernel_grads, summed_back.astype(jnp.bfloat16))
    weight_grad, input_grad = lax.scan(backward_device, jnp.zeros((OFFSETS, C, C), jnp.float32), (voxels, grad_ext, sources, targets))
    return (activated.reshape(SCANS, VOXELS, C), input_grad.reshape(SCANS, VOXELS, C), weight_grad, gain_grad, shift_grad)
```

```python
import jax
import jax.numpy as jnp
from jax import lax
from jax.experimental import pallas as pl
from jax.experimental.pallas import tpu as pltpu
from jax.sharding import PartitionSpec as P

GRID_W = 8
DIRECTIONS = ((-1, -1), (-1, 0), (-1, 1), (0, -1), (0, 1), (1, -1), (1, 0), (1, 1))
EPSILON = 1e-05
LANES = 128
CHAINS = 8
GATHER_UNROLL = 32
SCATTER_UNROLL = 4
VMEM_LIMIT = 60 << 20


def live_directions(regions):
    rows = regions // GRID_W
    return [j for j, (dr, dc) in enumerate(DIRECTIONS) if abs(dr) < rows and abs(dc) < GRID_W]


def neighbour_pairs(regions, step):
    rows = regions // GRID_W
    pairs = []
    for r in range(regions):
        row, col = r // GRID_W + step[0], r % GRID_W + step[1]
        if 0 <= row < rows and 0 <= col < GRID_W:
            pairs.append((r, row * GRID_W + col))
    return pairs


def fill_table(table, first, rows):
    count, channels = rows.shape
    rows = rows.astype(jnp.float32)
    table[pl.ds(2 * first, count, stride=2), :] = rows[:, :LANES]
    rest = jnp.concatenate(
        [rows[:, LANES:], jnp.zeros((count, 2 * LANES - channels), jnp.float32)], axis=1
    )
    table[pl.ds(2 * first + 1, count, stride=2), :] = rest


def gather_rows(index, table, buffer, pairs):
    @pl.loop(0, pairs, step=GATHER_UNROLL)
    def _(start):
        for u in range(GATHER_UNROLL):
            source = pl.multiple_of(index[0, 0, start + u] * 2, 2)
            target = pl.multiple_of((start + u) * 2, 2)
            buffer[pl.ds(target, 2), :] = table[pl.ds(source, 2), :]


def scatter_rows(index, buffer, sums, pairs):
    per_chain = pairs // CHAINS

    @pl.loop(0, per_chain, step=SCATTER_UNROLL)
    def _(start):
        for u in range(SCATTER_UNROLL):
            for chain in range(CHAINS):
                pair = chain * per_chain + start + u
                target = pl.multiple_of(index[0, 0, pair] * 2, 2)
                source = pl.multiple_of(pair * 2, 2)
                sums[chain][pl.ds(target, 2), :] += buffer[pl.ds(source, 2), :]


def joined(buffer, pairs, channels):
    low = buffer[pl.ds(0, pairs, stride=2), :]
    high = buffer[pl.ds(1, pairs, stride=2), :]
    return jnp.concatenate([low, high[:, : channels - LANES]], axis=1)


def chain_total(sums, first, count, channels):
    low = sums[0][pl.ds(2 * first, count, stride=2), :]
    high = sums[0][pl.ds(2 * first + 1, count, stride=2), :]
    for part in sums[1:]:
        low += part[pl.ds(2 * first, count, stride=2), :]
        high += part[pl.ds(2 * first + 1, count, stride=2), :]
    return jnp.concatenate([low, high[:, : channels - LANES]], axis=1)


def round_up(n, m):
    return (n + m - 1) // m * m


def forward_conv(features, weight, sources, targets, live, slots):
    rows, channels = features.shape
    offsets, _, pairs = sources.shape
    extended = round_up(rows + 8 * slots + 1, 8)
    ndir = len(live)

    def kernel(src_ref, dst_ref, x_ref, w_ref, summed_ref, out_ref, kept_ref, table, gbuf, vbuf, *sums):
        k = pl.program_id(0)

        @pl.when(k == 0)
        def _():
            fill_table(table, 0, x_ref[...])
            vbuf[...] = jnp.zeros_like(vbuf)
            for part in sums:
                part[...] = jnp.zeros_like(part)

        gather_rows(src_ref, table, gbuf, pairs)
        picked = joined(gbuf, pairs, channels).astype(jnp.bfloat16)
        kept_ref[0] = picked
        product = jnp.dot(picked, w_ref[0], preferred_element_type=jnp.float32)
        fill_table(vbuf, 0, product)
        scatter_rows(dst_ref, vbuf, sums, pairs)

        @pl.when(k == offsets - 1)
        def _():
            for first in range(0, rows, 256):
                summed_ref[pl.ds(first, 256), :] = chain_total(sums, first, 256, channels)
            for place, j in enumerate(live):
                out_ref[place] = chain_total(sums, rows + j * slots, slots, channels).astype(
                    jnp.bfloat16
                )

    smem = lambda: pl.BlockSpec((1, 1, pairs), lambda k: (k, 0, 0), memory_space=pltpu.SMEM)
    return pl.pallas_call(
        kernel,
        grid=(offsets,),
        in_specs=[
            smem(),
            smem(),
            pl.BlockSpec((rows, channels), lambda k: (0, 0)),
            pl.BlockSpec((1, channels, channels), lambda k: (k, 0, 0)),
        ],
        out_specs=[
            pl.BlockSpec((rows, channels), lambda k: (0, 0)),
            pl.BlockSpec((ndir, slots, channels), lambda k: (0, 0, 0)),
            pl.BlockSpec((1, pairs, channels), lambda k: (k, 0, 0)),
        ],
        out_shape=[
            jax.ShapeDtypeStruct((rows, channels), jnp.float32),
            jax.ShapeDtypeStruct((ndir, slots, channels), jnp.bfloat16),
            jax.ShapeDtypeStruct((offsets, pairs, channels), jnp.bfloat16),
        ],
        scratch_shapes=[
            pltpu.VMEM((2 * rows, LANES), jnp.float32),
            pltpu.VMEM((2 * pairs, LANES), jnp.float32),
            pltpu.VMEM((2 * pairs, LANES), jnp.float32),
        ]
        + [pltpu.VMEM((2 * extended, LANES), jnp.float32)] * CHAINS,
        compiler_params=pltpu.CompilerParams(vmem_limit_bytes=VMEM_LIMIT),
        name="forward_conv",
    )(sources, targets, features, weight)


def backward_conv(pre_grad, returned, kept, weight, sources, targets, live, slots):
    rows, channels = pre_grad.shape
    offsets, _, pairs = sources.shape
    extended = round_up(rows + 8 * slots + 1, 8)
    ndir = len(live)

    def kernel(src_ref, dst_ref, g_ref, ret_ref, x_ref, w_ref, wgrad_ref, xgrad_ref, table, gbuf, vbuf, *sums):
        k = pl.program_id(0)

        @pl.when(k == 0)
        def _():
            fill_table(table, 0, g_ref[...])
            for place, j in enumerate(live):
                fill_table(table, rows + j * slots, ret_ref[place])
            tail = 2 * (rows + 8 * slots)
            table[tail:, :] = jnp.zeros((2 * extended - tail, LANES), jnp.float32)
            vbuf[...] = jnp.zeros_like(vbuf)
            for part in sums:
                part[...] = jnp.zeros_like(part)

        gather_rows(dst_ref, table, gbuf, pairs)
        picked = joined(gbuf, pairs, channels).astype(jnp.bfloat16)
        wgrad_ref[0] = lax.dot_general(
            x_ref[0], picked, (((0,), (0,)), ((), ())), preferred_element_type=jnp.float32
        )
        product = lax.dot_general(
            picked, w_ref[0], (((1,), (1,)), ((), ())), preferred_element_type=jnp.float32
        )
        fill_table(vbuf, 0, product)
        scatter_rows(src_ref, vbuf, sums, pairs)

        @pl.when(k == offsets - 1)
        def _():
            for first in range(0, rows, 256):
                xgrad_ref[pl.ds(first, 256), :] = chain_total(sums, first, 256, channels).astype(
                    jnp.bfloat16
                )

    smem = lambda: pl.BlockSpec((1, 1, pairs), lambda k: (k, 0, 0), memory_space=pltpu.SMEM)
    return pl.pallas_call(
        kernel,
        grid=(offsets,),
        in_specs=[
            smem(),
            smem(),
            pl.BlockSpec((rows, channels), lambda k: (0, 0)),
            pl.BlockSpec((ndir, slots, channels), lambda k: (0, 0, 0)),
            pl.BlockSpec((1, pairs, channels), lambda k: (k, 0, 0)),
            pl.BlockSpec((1, channels, channels), lambda k: (k, 0, 0)),
        ],
        out_specs=[
            pl.BlockSpec((1, channels, channels), lambda k: (k, 0, 0)),
            pl.BlockSpec((rows, channels), lambda k: (0, 0)),
        ],
        out_shape=[
            jax.ShapeDtypeStruct((offsets, channels, channels), jnp.float32),
            jax.ShapeDtypeStruct((rows, channels), jnp.bfloat16),
        ],
        scratch_shapes=[
            pltpu.VMEM((2 * extended, LANES), jnp.float32),
            pltpu.VMEM((2 * pairs, LANES), jnp.float32),
            pltpu.VMEM((2 * pairs, LANES), jnp.float32),
        ]
        + [pltpu.VMEM((2 * rows, LANES), jnp.float32)] * CHAINS,
        compiler_params=pltpu.CompilerParams(vmem_limit_bytes=VMEM_LIMIT),
        name="backward_conv",
    )(sources, targets, pre_grad, returned, kept, weight)


def on_device(
    features, weight, norm_gain, norm_shift, cotangent, counts, in_rows, out_slots, land_rows
):
    regions = lax.axis_size("region")
    live = live_directions(regions)
    voxels = features[0]
    row_count, channels = voxels.shape
    from_all = in_rows[0, 0][:, None, :]
    to_all = out_slots[0, 0][:, None, :]
    slot_count = land_rows.shape[3]
    places = jnp.concatenate([land_rows[0, 0, j] for j in live])
    summed, outgoing, kept = forward_conv(voxels, weight, from_all, to_all, live, slot_count)
    arrived = jnp.concatenate(
        [
            lax.ppermute(outgoing[place], "region", neighbour_pairs(regions, DIRECTIONS[j]))
            for place, j in enumerate(live)
        ]
    )
    preact = summed.at[places].add(arrived.astype(jnp.float32))
    alive = (lax.broadcasted_iota(jnp.int32, (row_count, 1), 0) < counts[0, 0]).astype(jnp.float32)
    own_count = counts[0, 0].astype(jnp.float32)
    column_sum, count_total = lax.psum(
        (jnp.sum(preact * alive, axis=0), own_count), ("region", "dp")
    )
    average = column_sum / count_total
    centered = (preact - average) * alive
    variance = lax.psum(jnp.sum(centered * centered, axis=0), ("region", "dp")) / count_total
    inverse = lax.rsqrt(variance + EPSILON)
    normed = (preact - average) * inverse
    shifted = norm_gain * normed + norm_shift
    sigma = jax.nn.sigmoid(shifted)
    slope = sigma * (1.0 + shifted * (1.0 - sigma)) * alive
    activated = (shifted * sigma * alive).astype(jnp.bfloat16)
    upstream = cotangent[0].astype(jnp.float32) * slope
    gain_grad, shift_grad = lax.psum(
        (jnp.sum(upstream * normed, axis=0), jnp.sum(upstream, axis=0)), ("region", "dp")
    )
    pre_grad = (
        norm_gain
        * inverse
        * (upstream - shift_grad / count_total - normed * gain_grad / count_total)
        * alive
    ).astype(jnp.bfloat16)
    picked = pre_grad[places].reshape(len(live), slot_count, channels)
    returned = jnp.stack(
        [
            lax.ppermute(
                picked[place],
                "region",
                [(b, a) for a, b in neighbour_pairs(regions, DIRECTIONS[j])],
            )
            for place, j in enumerate(live)
        ]
    )
    kernel_grads, input_grad = backward_conv(
        pre_grad, returned, kept, weight, from_all, to_all, live, slot_count
    )
    weight_grad = lax.psum(kernel_grads, ("region", "dp"))
    return (activated[None], input_grad[None], weight_grad, gain_grad, shift_grad)


def solution(mesh):
    return jax.shard_map(
        on_device,
        mesh=mesh,
        in_specs=(
            P("dp", "region", None),
            P(),
            P(),
            P(),
            P("dp", "region", None),
            P("dp", "region"),
            P("dp", "region", None, None),
            P("dp", "region", None, None),
            P("dp", "region", None, None),
        ),
        out_specs=(P("dp", "region", None), P("dp", "region", None), P(), P(), P()),
        check_vma=False,
    )
```

```python
import jax
import jax.numpy as jnp
from jax import lax
from jax.experimental import pallas as pl
from jax.experimental.pallas import tpu as pltpu
from jax.sharding import PartitionSpec as P

GRID_W = 8
DIRECTIONS = ((-1, -1), (-1, 0), (-1, 1), (0, -1), (0, 1), (1, -1), (1, 0), (1, 1))
EPSILON = 1e-05
LANES = 128
CHAINS = 8
SCATTER_UNROLL = 8
VMEM_LIMIT = 60 << 20


def live_directions(regions):
    rows = regions // GRID_W
    return [j for j, (dr, dc) in enumerate(DIRECTIONS) if abs(dr) < rows and abs(dc) < GRID_W]


def neighbour_pairs(regions, step):
    rows = regions // GRID_W
    pairs = []
    for r in range(regions):
        row, col = r // GRID_W + step[0], r % GRID_W + step[1]
        if 0 <= row < rows and 0 <= col < GRID_W:
            pairs.append((r, row * GRID_W + col))
    return pairs


def fill_table(table, first, rows):
    count, channels = rows.shape
    rows = rows.astype(jnp.float32)
    table[pl.ds(2 * first, count, stride=2), :] = rows[:, :LANES]
    rest = jnp.concatenate(
        [rows[:, LANES:], jnp.zeros((count, 2 * LANES - channels), jnp.float32)], axis=1
    )
    table[pl.ds(2 * first + 1, count, stride=2), :] = rest


def gather_and_scatter(gather_index, table, gbuf, scatter_index, vbuf, sums, pairs):
    per_chain = pairs // CHAINS

    @pl.loop(0, per_chain, step=SCATTER_UNROLL)
    def _(start):
        for u in range(SCATTER_UNROLL):
            for chain in range(CHAINS):
                pair = chain * per_chain + start + u
                place = pl.multiple_of(pair * 2, 2)
                target = pl.multiple_of(scatter_index[0, 0, pair] * 2, 2)
                sums[chain][pl.ds(target, 2), :] += vbuf[pl.ds(place, 2), :]
                source = pl.multiple_of(gather_index[0, 0, pair] * 2, 2)
                gbuf[pl.ds(place, 2), :] = table[pl.ds(source, 2), :]


def joined(buffer, pairs, channels):
    low = buffer[pl.ds(0, pairs, stride=2), :]
    high = buffer[pl.ds(1, pairs, stride=2), :]
    return jnp.concatenate([low, high[:, : channels - LANES]], axis=1)


def chain_total(sums, first, count, channels):
    low = sums[0][pl.ds(2 * first, count, stride=2), :]
    high = sums[0][pl.ds(2 * first + 1, count, stride=2), :]
    for part in sums[1:]:
        low += part[pl.ds(2 * first, count, stride=2), :]
        high += part[pl.ds(2 * first + 1, count, stride=2), :]
    return jnp.concatenate([low, high[:, : channels - LANES]], axis=1)


def round_up(n, m):
    return (n + m - 1) // m * m


def packed_rows(channels):
    return channels + channels // 2


def doubling_steps():
    steps = []
    for axis in ("dp", "region"):
        stride = 1
        while stride < lax.axis_size(axis):
            steps.append((stride, axis))
            stride *= 2
    return [(axis, stride) for stride, axis in sorted(steps)]


def exchange(value, axis, stride):
    return lax.ppermute(value, axis, [(i, i ^ stride) for i in range(lax.axis_size(axis))])


def all_sum(value):
    for axis, stride in doubling_steps():
        value = value + exchange(value, axis, stride)
    return value


def all_moments(count, mean, square):
    value = jnp.stack([jnp.broadcast_to(count, mean.shape), mean, square])
    for axis, stride in doubling_steps():
        other = exchange(value, axis, stride)
        total = value[0] + other[0]
        gap = other[1] - value[1]
        value = jnp.stack(
            [
                total,
                (value[0] * value[1] + other[0] * other[1]) / total,
                value[2] + other[2] + gap * gap * (value[0] * other[0] / total),
            ]
        )
    return value[0], value[1], value[2]


def sum_over_devices(value):
    steps = doubling_steps()
    for axis, stride in steps:
        half = value.shape[0] // 2
        upper = (lax.axis_index(axis) // stride) % 2
        sent = lax.dynamic_slice_in_dim(value, (1 - upper) * half, half, 0)
        kept = lax.dynamic_slice_in_dim(value, upper * half, half, 0)
        value = kept + exchange(sent.astype(jnp.bfloat16), axis, stride).astype(jnp.float32)
    value = value.astype(jnp.bfloat16)
    for axis, stride in reversed(steps):
        upper = (lax.axis_index(axis) // stride) % 2 == 1
        other = exchange(value, axis, stride)
        value = jnp.concatenate(
            [jnp.where(upper, other, value), jnp.where(upper, value, other)], axis=0
        )
    return value


def unpack_matrices(packed, offsets, channels):
    height = packed_rows(channels)
    rest = channels - LANES

    def kernel(in_ref, out_ref):
        value = in_ref[...].astype(jnp.float32)
        out_ref[0, :, :LANES] = value[:channels]
        out_ref[0, : channels // 2, LANES:] = value[channels:, :rest]
        out_ref[0, channels // 2 :, LANES:] = value[channels:, rest:]

    return pl.pallas_call(
        kernel,
        grid=(offsets,),
        in_specs=[pl.BlockSpec((height, LANES), lambda k: (k, 0))],
        out_specs=pl.BlockSpec((1, channels, channels), lambda k: (k, 0, 0)),
        out_shape=jax.ShapeDtypeStruct((offsets, channels, channels), jnp.float32),
        name="unpack_matrices",
    )(packed)


def forward_conv(features, weight, sources, targets, live, slots):
    rows, channels = features.shape
    offsets, _, pairs = sources.shape
    extended = round_up(rows + 8 * slots + 1, 8)
    ndir = len(live)

    def kernel(src_ref, dst_ref, x_ref, w_ref, summed_ref, out_ref, kept_ref, table, gbuf, vbuf, *sums):
        k = pl.program_id(0)

        @pl.when(k == 0)
        def _():
            fill_table(table, 0, x_ref[...])
            vbuf[...] = jnp.zeros_like(vbuf)
            for part in sums:
                part[...] = jnp.zeros_like(part)

        gather_and_scatter(src_ref, table, gbuf, dst_ref, vbuf, sums, pairs)
        picked = joined(gbuf, pairs, channels).astype(jnp.bfloat16)
        kept_ref[0] = picked
        product = jnp.dot(picked, w_ref[0], preferred_element_type=jnp.float32)
        fill_table(vbuf, 0, product)

        @pl.when(k == offsets)
        def _():
            for first in range(0, rows, 256):
                summed_ref[pl.ds(first, 256), :] = chain_total(sums, first, 256, channels)
            for place, j in enumerate(live):
                out_ref[place] = chain_total(sums, rows + j * slots, slots, channels).astype(
                    jnp.bfloat16
                )

    now = lambda k: (jnp.minimum(k, offsets - 1), 0, 0)
    before = lambda k: (jnp.maximum(k - 1, 0), 0, 0)
    smem = lambda where: pl.BlockSpec((1, 1, pairs), where, memory_space=pltpu.SMEM)
    return pl.pallas_call(
        kernel,
        grid=(offsets + 1,),
        in_specs=[
            smem(now),
            smem(before),
            pl.BlockSpec((rows, channels), lambda k: (0, 0)),
            pl.BlockSpec((1, channels, channels), now),
        ],
        out_specs=[
            pl.BlockSpec((rows, channels), lambda k: (0, 0)),
            pl.BlockSpec((ndir, slots, channels), lambda k: (0, 0, 0)),
            pl.BlockSpec((1, pairs, channels), now),
        ],
        out_shape=[
            jax.ShapeDtypeStruct((rows, channels), jnp.float32),
            jax.ShapeDtypeStruct((ndir, slots, channels), jnp.bfloat16),
            jax.ShapeDtypeStruct((offsets, pairs, channels), jnp.bfloat16),
        ],
        scratch_shapes=[
            pltpu.VMEM((2 * rows, LANES), jnp.float32),
            pltpu.VMEM((2 * pairs, LANES), jnp.float32),
            pltpu.VMEM((2 * pairs, LANES), jnp.float32),
        ]
        + [pltpu.VMEM((2 * extended, LANES), jnp.float32)] * CHAINS,
        compiler_params=pltpu.CompilerParams(vmem_limit_bytes=VMEM_LIMIT),
        name="forward_conv",
    )(sources, targets, features, weight)


def backward_conv(pre_grad, returned, kept, weight, sources, targets, live, slots):
    rows, channels = pre_grad.shape
    offsets, _, pairs = sources.shape
    extended = round_up(rows + 8 * slots + 1, 8)
    ndir = len(live)

    def kernel(src_ref, dst_ref, g_ref, ret_ref, x_ref, w_ref, wgrad_ref, xgrad_ref, table, gbuf, vbuf, *sums):
        k = pl.program_id(0)

        @pl.when(k == 0)
        def _():
            fill_table(table, 0, g_ref[...])
            for place, j in enumerate(live):
                fill_table(table, rows + j * slots, ret_ref[place])
            tail = 2 * (rows + 8 * slots)
            table[tail:, :] = jnp.zeros((2 * extended - tail, LANES), jnp.float32)
            vbuf[...] = jnp.zeros_like(vbuf)
            for part in sums:
                part[...] = jnp.zeros_like(part)

        gather_and_scatter(dst_ref, table, gbuf, src_ref, vbuf, sums, pairs)
        picked = joined(gbuf, pairs, channels).astype(jnp.bfloat16)
        wgrad = lax.dot_general(
            x_ref[0], picked, (((0,), (0,)), ((), ())), preferred_element_type=jnp.float32
        )
        wgrad_ref[:channels, :] = wgrad[:, :LANES]
        wgrad_ref[channels:, :] = jnp.concatenate(
            [wgrad[: channels // 2, LANES:], wgrad[channels // 2 :, LANES:]], axis=1
        )
        product = lax.dot_general(
            picked, w_ref[0], (((1,), (1,)), ((), ())), preferred_element_type=jnp.float32
        )
        fill_table(vbuf, 0, product)

        @pl.when(k == offsets)
        def _():
            for first in range(0, rows, 256):
                xgrad_ref[pl.ds(first, 256), :] = chain_total(sums, first, 256, channels).astype(
                    jnp.bfloat16
                )

    now = lambda k: (jnp.minimum(k, offsets - 1), 0, 0)
    before = lambda k: (jnp.maximum(k - 1, 0), 0, 0)
    smem = lambda where: pl.BlockSpec((1, 1, pairs), where, memory_space=pltpu.SMEM)
    return pl.pallas_call(
        kernel,
        grid=(offsets + 1,),
        in_specs=[
            smem(before),
            smem(now),
            pl.BlockSpec((rows, channels), lambda k: (0, 0)),
            pl.BlockSpec((ndir, slots, channels), lambda k: (0, 0, 0)),
            pl.BlockSpec((1, pairs, channels), now),
            pl.BlockSpec((1, channels, channels), now),
        ],
        out_specs=[
            pl.BlockSpec((packed_rows(channels), LANES), lambda k: (jnp.minimum(k, offsets - 1), 0)),
            pl.BlockSpec((rows, channels), lambda k: (0, 0)),
        ],
        out_shape=[
            jax.ShapeDtypeStruct((round_up(offsets * packed_rows(channels), 4096), LANES), jnp.float32),
            jax.ShapeDtypeStruct((rows, channels), jnp.bfloat16),
        ],
        scratch_shapes=[
            pltpu.VMEM((2 * extended, LANES), jnp.float32),
            pltpu.VMEM((2 * pairs, LANES), jnp.float32),
            pltpu.VMEM((2 * pairs, LANES), jnp.float32),
        ]
        + [pltpu.VMEM((2 * rows, LANES), jnp.float32)] * CHAINS,
        compiler_params=pltpu.CompilerParams(vmem_limit_bytes=VMEM_LIMIT),
        name="backward_conv",
    )(sources, targets, pre_grad, returned, kept, weight)


def on_device(
    features, weight, norm_gain, norm_shift, cotangent, counts, in_rows, out_slots, land_rows
):
    regions = lax.axis_size("region")
    live = live_directions(regions)
    voxels = features[0]
    row_count, channels = voxels.shape
    from_all = in_rows[0, 0][:, None, :]
    to_all = out_slots[0, 0][:, None, :]
    slot_count = land_rows.shape[3]
    places = jnp.concatenate([land_rows[0, 0, j] for j in live])
    summed, outgoing, kept = forward_conv(voxels, weight, from_all, to_all, live, slot_count)
    arrived = jnp.concatenate(
        [
            lax.ppermute(outgoing[place], "region", neighbour_pairs(regions, DIRECTIONS[j]))
            for place, j in enumerate(live)
        ]
    )
    preact = summed.at[places].add(arrived.astype(jnp.float32))
    alive = (lax.broadcasted_iota(jnp.int32, (row_count, 1), 0) < counts[0, 0]).astype(jnp.float32)
    own_count = counts[0, 0].astype(jnp.float32)
    own_mean = jnp.sum(preact * alive, axis=0) / own_count
    own_centered = (preact - own_mean) * alive
    count_total, average, square = all_moments(
        own_count, own_mean, jnp.sum(own_centered * own_centered, axis=0)
    )
    variance = square / count_total
    inverse = lax.rsqrt(variance + EPSILON)
    normed = (preact - average) * inverse
    shifted = norm_gain * normed + norm_shift
    sigma = jax.nn.sigmoid(shifted)
    slope = sigma * (1.0 + shifted * (1.0 - sigma)) * alive
    activated = (shifted * sigma * alive).astype(jnp.bfloat16)
    upstream = cotangent[0].astype(jnp.float32) * slope
    gain_grad, shift_grad = all_sum(
        jnp.stack([jnp.sum(upstream * normed, axis=0), jnp.sum(upstream, axis=0)])
    )
    pre_grad = (
        norm_gain
        * inverse
        * (upstream - shift_grad / count_total - normed * gain_grad / count_total)
        * alive
    ).astype(jnp.bfloat16)
    picked = pre_grad[places].reshape(len(live), slot_count, channels)
    returned = jnp.stack(
        [
            lax.ppermute(
                picked[place],
                "region",
                [(b, a) for a, b in neighbour_pairs(regions, DIRECTIONS[j])],
            )
            for place, j in enumerate(live)
        ]
    )
    kernel_grads, input_grad = backward_conv(
        pre_grad, returned, kept, weight, from_all, to_all, live, slot_count
    )
    weight_grad = unpack_matrices(sum_over_devices(kernel_grads), weight.shape[0], channels)
    return (activated[None], input_grad[None], weight_grad, gain_grad, shift_grad)


def solution(mesh):
    return jax.shard_map(
        on_device,
        mesh=mesh,
        in_specs=(
            P("dp", "region", None),
            P(),
            P(),
            P(),
            P("dp", "region", None),
            P("dp", "region"),
            P("dp", "region", None, None),
            P("dp", "region", None, None),
            P("dp", "region", None, None),
        ),
        out_specs=(P("dp", "region", None), P("dp", "region", None), P(), P(), P()),
        check_vma=False,
    )
```

```python
import jax
import jax.numpy as jnp
from jax import lax
from jax.experimental import pallas as pl
from jax.experimental.pallas import tpu as pltpu
from jax.sharding import PartitionSpec as P

GRID_W = 8
DIRECTIONS = ((-1, -1), (-1, 0), (-1, 1), (0, -1), (0, 1), (1, -1), (1, 0), (1, 1))
EPSILON = 1e-05
LANES = 128
CHAINS = 8
SCATTER_UNROLL = 8
HALF_ROWS = 4096
UNPACK = 7
VMEM_LIMIT = 60 << 20


def live_directions(regions):
    rows = regions // GRID_W
    return [j for j, (dr, dc) in enumerate(DIRECTIONS) if abs(dr) < rows and abs(dc) < GRID_W]


def neighbour_pairs(regions, step):
    rows = regions // GRID_W
    pairs = []
    for r in range(regions):
        row, col = r // GRID_W + step[0], r % GRID_W + step[1]
        if 0 <= row < rows and 0 <= col < GRID_W:
            pairs.append((r, row * GRID_W + col))
    return pairs


def fill_table(table, first, rows):
    count, channels = rows.shape
    rows = rows.astype(jnp.float32)
    table[pl.ds(2 * first, count, stride=2), :] = rows[:, :LANES]
    rest = jnp.concatenate(
        [rows[:, LANES:], jnp.zeros((count, 2 * LANES - channels), jnp.float32)], axis=1
    )
    table[pl.ds(2 * first + 1, count, stride=2), :] = rest


def gather_and_scatter(gather_index, table, gbuf, scatter_index, vbuf, sums, pairs):
    per_chain = pairs // CHAINS

    @pl.loop(0, per_chain, step=SCATTER_UNROLL)
    def _(start):
        for u in range(SCATTER_UNROLL):
            for chain in range(CHAINS):
                pair = chain * per_chain + start + u
                place = pl.multiple_of(pair * 2, 2)
                target = pl.multiple_of(scatter_index[0, 0, pair], 2)
                sums[chain][pl.ds(target, 2), :] += vbuf[pl.ds(place, 2), :]
                source = pl.multiple_of(gather_index[0, 0, pair], 2)
                gbuf[pl.ds(place, 2), :] = table[pl.ds(source, 2), :]


def joined(buffer, pairs, channels):
    low = buffer[pl.ds(0, pairs, stride=2), :]
    high = buffer[pl.ds(1, pairs, stride=2), :]
    return jnp.concatenate([low, high[:, : channels - LANES]], axis=1)


def chain_total(sums, first, count, channels):
    low = sums[0][pl.ds(2 * first, count, stride=2), :]
    high = sums[0][pl.ds(2 * first + 1, count, stride=2), :]
    for part in sums[1:]:
        low += part[pl.ds(2 * first, count, stride=2), :]
        high += part[pl.ds(2 * first + 1, count, stride=2), :]
    return jnp.concatenate([low, high[:, : channels - LANES]], axis=1)


def round_up(n, m):
    return (n + m - 1) // m * m


def packed_rows(channels):
    return channels + channels // 2


def doubling_steps():
    steps = []
    for axis in ("dp", "region"):
        stride = 1
        while stride < lax.axis_size(axis):
            steps.append((stride, axis))
            stride *= 2
    return [(axis, stride) for stride, axis in sorted(steps)]


def exchange(value, axis, stride):
    return lax.ppermute(value, axis, [(i, i ^ stride) for i in range(lax.axis_size(axis))])


def all_sum(value):
    for axis, stride in doubling_steps():
        value = value + exchange(value, axis, stride)
    return value


def all_moments(count, mean, square):
    value = jnp.stack([jnp.broadcast_to(count, mean.shape), mean, square])
    for axis, stride in doubling_steps():
        other = exchange(value, axis, stride)
        total = value[0] + other[0]
        gap = other[1] - value[1]
        value = jnp.stack(
            [
                total,
                (value[0] * value[1] + other[0] * other[1]) / total,
                value[2] + other[2] + gap * gap * (value[0] * other[0] / total),
            ]
        )
    return value[0], value[1], value[2]


def reduction_rounds():
    steps = doubling_steps()
    return [steps[:1]] + [steps[i : i + 2] for i in range(1, len(steps), 2)]


def place_in(group):
    place = 0
    for bit, (axis, stride) in enumerate(group):
        place = place + (lax.axis_index(axis) // stride) % 2 * (1 << bit)
    inner = lax.axis_size("dp")
    count = inner * lax.axis_size("region")
    permutations = []
    for mask in range(1, 1 << len(group)):
        flip = 0
        for bit, (axis, stride) in enumerate(group):
            if mask >> bit & 1:
                flip ^= stride * (inner if axis == "region" else 1)
        permutations.append((mask, [(i, i ^ flip) for i in range(count)]))
    return place, permutations


def sent_shares(value, group):
    place, permutations = place_in(group)
    share = value.shape[0] >> len(group)
    return [
        lax.dynamic_slice_in_dim(value, (place ^ mask) * share, share, 0).astype(jnp.bfloat16)
        for mask, _ in permutations
    ]


def sum_share(value, sent, group):
    place, permutations = place_in(group)
    share = value.shape[0] >> len(group)
    total = lax.dynamic_slice_in_dim(value, place * share, share, 0)
    for part, (_, permutation) in zip(sent, permutations):
        got = lax.ppermute(part, ("region", "dp"), permutation)
        total = total + got.astype(jnp.float32)
    return total


def gathered_shares(value, group):
    place, permutations = place_in(group)
    shares = [value] + [
        lax.ppermute(value, ("region", "dp"), permutation) for _, permutation in permutations
    ]
    ordered = []
    for position in range(len(shares)):
        chosen = shares[position]
        for own in range(1, len(shares)):
            chosen = jnp.where(place == own, shares[own ^ position], chosen)
        ordered.append(chosen)
    return jnp.concatenate(ordered, axis=0)


def unpack_matrices(own, other, place, offsets, channels):
    height = packed_rows(channels)
    rest = channels - LANES
    half = round_up(offsets, 2) // 2

    def kernel(place_ref, own_ref, other_ref, out_ref):
        def write(value, position):
            out_ref[position, :, :LANES] = value[:channels]
            out_ref[position, : channels // 2, LANES:] = value[channels:, :rest]
            out_ref[position, channels // 2 :, LANES:] = value[channels:, rest:]

        @pl.when(place_ref[pl.program_id(0)] == 1)
        def _():
            for position in range(UNPACK):
                write(own_ref[position * height : (position + 1) * height].astype(jnp.float32), position)

        @pl.when(place_ref[pl.program_id(0)] == 0)
        def _():
            for position in range(UNPACK):
                write(other_ref[position * height : (position + 1) * height].astype(jnp.float32), position)

    steps = half // UNPACK
    block = lambda k, place: (k % steps, 0)
    mine = jnp.repeat(jnp.stack([place == 0, place == 1]), steps).astype(jnp.int32)
    return pl.pallas_call(
        kernel,
        grid_spec=pltpu.PrefetchScalarGridSpec(
            num_scalar_prefetch=1,
            grid=(2 * steps,),
            in_specs=[pl.BlockSpec((UNPACK * height, LANES), block)] * 2,
            out_specs=pl.BlockSpec((UNPACK, channels, channels), lambda k, place: (k, 0, 0)),
        ),
        out_shape=jax.ShapeDtypeStruct((offsets, channels, channels), jnp.float32),
        name="unpack_matrices",
    )(mine, own, other)


def forward_conv(features, weight, sources, targets, live, slots):
    rows, channels = features.shape
    offsets, _, pairs = sources.shape
    extended = round_up(rows + 8 * slots + 1, 8)
    ndir = len(live)

    def kernel(src_ref, dst_ref, x_ref, w_ref, summed_ref, out_ref, kept_ref, table, gbuf, vbuf, *sums):
        k = pl.program_id(0)

        @pl.when(k == 0)
        def _():
            fill_table(table, 0, x_ref[...])
            vbuf[...] = jnp.zeros_like(vbuf)
            for part in sums:
                part[...] = jnp.zeros_like(part)

        gather_and_scatter(src_ref, table, gbuf, dst_ref, vbuf, sums, pairs)
        picked = joined(gbuf, pairs, channels).astype(jnp.bfloat16)
        kept_ref[0] = picked
        product = jnp.dot(picked, w_ref[0], preferred_element_type=jnp.float32)
        fill_table(vbuf, 0, product)

        @pl.when(k == offsets)
        def _():
            for first in range(0, rows, 256):
                summed_ref[pl.ds(first, 256), :] = chain_total(sums, first, 256, channels)
            for place, j in enumerate(live):
                out_ref[place] = chain_total(sums, rows + j * slots, slots, channels).astype(
                    jnp.bfloat16
                )

    now = lambda k: (jnp.minimum(k, offsets - 1), 0, 0)
    before = lambda k: (jnp.maximum(k - 1, 0), 0, 0)
    smem = lambda where: pl.BlockSpec((1, 1, pairs), where, memory_space=pltpu.SMEM)
    return pl.pallas_call(
        kernel,
        grid=(offsets + 1,),
        in_specs=[
            smem(now),
            smem(before),
            pl.BlockSpec((rows, channels), lambda k: (0, 0)),
            pl.BlockSpec((1, channels, channels), now),
        ],
        out_specs=[
            pl.BlockSpec((rows, channels), lambda k: (0, 0)),
            pl.BlockSpec((ndir, slots, channels), lambda k: (0, 0, 0)),
            pl.BlockSpec((1, pairs, channels), now),
        ],
        out_shape=[
            jax.ShapeDtypeStruct((rows, channels), jnp.float32),
            jax.ShapeDtypeStruct((ndir, slots, channels), jnp.bfloat16),
            jax.ShapeDtypeStruct((offsets, pairs, channels), jnp.bfloat16),
        ],
        scratch_shapes=[
            pltpu.VMEM((2 * rows, LANES), jnp.float32),
            pltpu.VMEM((2 * pairs, LANES), jnp.float32),
            pltpu.VMEM((2 * pairs, LANES), jnp.float32),
        ]
        + [pltpu.VMEM((2 * extended, LANES), jnp.float32)] * CHAINS,
        compiler_params=pltpu.CompilerParams(vmem_limit_bytes=VMEM_LIMIT),
        name="forward_conv",
    )(sources, targets, features, weight)


def backward_conv(pre_grad, returned, kept, weight, sources, targets, live, slots):
    rows, channels = pre_grad.shape
    offsets, _, pairs = sources.shape
    extended = round_up(rows + 8 * slots + 1, 8)
    ndir = len(live)
    height = packed_rows(channels)
    half = round_up(offsets, 2) // 2
    half_rows = round_up(half * height, HALF_ROWS)

    def kernel(src_ref, dst_ref, g_ref, ret_ref, x_ref, w_ref, wgrad_ref, xgrad_ref, table, gbuf, vbuf, *sums):
        k = pl.program_id(0)

        @pl.when(k == 0)
        def _():
            fill_table(table, 0, g_ref[...])
            for place, j in enumerate(live):
                fill_table(table, rows + j * slots, ret_ref[place])
            tail = 2 * (rows + 8 * slots)
            table[tail:, :] = jnp.zeros((2 * extended - tail, LANES), jnp.float32)
            vbuf[...] = jnp.zeros_like(vbuf)
            wgrad_ref[half * height : half_rows, :] = jnp.zeros(
                (half_rows - half * height, LANES), jnp.float32
            )
            used = half_rows + (offsets - half) * height
            wgrad_ref[used:, :] = jnp.zeros((2 * half_rows - used, LANES), jnp.float32)
            for part in sums:
                part[...] = jnp.zeros_like(part)

        gather_and_scatter(dst_ref, table, gbuf, src_ref, vbuf, sums, pairs)
        picked = joined(gbuf, pairs, channels).astype(jnp.bfloat16)
        wgrad = lax.dot_general(
            x_ref[0], picked, (((0,), (0,)), ((), ())), preferred_element_type=jnp.float32
        )
        at = jnp.minimum(k, offsets - 1)
        first = jnp.where(at < half, at * height, half_rows + (at - half) * height)
        first = pl.multiple_of(first, 8)
        wgrad_ref[pl.ds(first, channels), :] = wgrad[:, :LANES]
        wgrad_ref[pl.ds(first + channels, channels // 2), :] = jnp.concatenate(
            [wgrad[: channels // 2, LANES:], wgrad[channels // 2 :, LANES:]], axis=1
        )
        product = lax.dot_general(
            picked, w_ref[0], (((1,), (1,)), ((), ())), preferred_element_type=jnp.float32
        )
        fill_table(vbuf, 0, product)

        @pl.when(k == offsets)
        def _():
            for first in range(0, rows, 256):
                xgrad_ref[pl.ds(first, 256), :] = chain_total(sums, first, 256, channels).astype(
                    jnp.bfloat16
                )

    now = lambda k: (jnp.minimum(k, offsets - 1), 0, 0)
    before = lambda k: (jnp.maximum(k - 1, 0), 0, 0)
    smem = lambda where: pl.BlockSpec((1, 1, pairs), where, memory_space=pltpu.SMEM)
    return pl.pallas_call(
        kernel,
        grid=(offsets + 1,),
        in_specs=[
            smem(before),
            smem(now),
            pl.BlockSpec((rows, channels), lambda k: (0, 0)),
            pl.BlockSpec((ndir, slots, channels), lambda k: (0, 0, 0)),
            pl.BlockSpec((1, pairs, channels), now),
            pl.BlockSpec((1, channels, channels), now),
        ],
        out_specs=[
            pl.BlockSpec((2 * half_rows, LANES), lambda k: (0, 0)),
            pl.BlockSpec((rows, channels), lambda k: (0, 0)),
        ],
        out_shape=[
            jax.ShapeDtypeStruct((2 * half_rows, LANES), jnp.float32),
            jax.ShapeDtypeStruct((rows, channels), jnp.bfloat16),
        ],
        scratch_shapes=[
            pltpu.VMEM((2 * extended, LANES), jnp.float32),
            pltpu.VMEM((2 * pairs, LANES), jnp.float32),
            pltpu.VMEM((2 * pairs, LANES), jnp.float32),
        ]
        + [pltpu.VMEM((2 * rows, LANES), jnp.float32)] * CHAINS,
        compiler_params=pltpu.CompilerParams(vmem_limit_bytes=VMEM_LIMIT),
        name="backward_conv",
    )(sources, targets, pre_grad, returned, kept, weight)


def on_device(
    features, weight, norm_gain, norm_shift, cotangent, counts, in_rows, out_slots, land_rows
):
    regions = lax.axis_size("region")
    live = live_directions(regions)
    voxels = features[0]
    row_count, channels = voxels.shape
    from_all = (in_rows[0, 0] * 2)[:, None, :]
    to_all = (out_slots[0, 0] * 2)[:, None, :]
    slot_count = land_rows.shape[3]
    places = jnp.concatenate([land_rows[0, 0, j] for j in live])
    summed, outgoing, kept = forward_conv(voxels, weight, from_all, to_all, live, slot_count)
    arrived = jnp.concatenate(
        [
            lax.ppermute(outgoing[place], "region", neighbour_pairs(regions, DIRECTIONS[j]))
            for place, j in enumerate(live)
        ]
    )
    preact = summed.at[places].add(arrived.astype(jnp.float32))
    alive = (lax.broadcasted_iota(jnp.int32, (row_count, 1), 0) < counts[0, 0]).astype(jnp.float32)
    own_count = counts[0, 0].astype(jnp.float32)
    own_mean = jnp.sum(preact * alive, axis=0) / own_count
    own_centered = (preact - own_mean) * alive
    count_total, average, square = all_moments(
        own_count, own_mean, jnp.sum(own_centered * own_centered, axis=0)
    )
    variance = square / count_total
    inverse = lax.rsqrt(variance + EPSILON)
    normed = (preact - average) * inverse
    shifted = norm_gain * normed + norm_shift
    sigma = jax.nn.sigmoid(shifted)
    slope = sigma * (1.0 + shifted * (1.0 - sigma)) * alive
    activated = (shifted * sigma * alive).astype(jnp.bfloat16)
    upstream = cotangent[0].astype(jnp.float32) * slope
    gain_grad, shift_grad = all_sum(
        jnp.stack([jnp.sum(upstream * normed, axis=0), jnp.sum(upstream, axis=0)])
    )
    pre_grad = (
        norm_gain
        * inverse
        * (upstream - shift_grad / count_total - normed * gain_grad / count_total)
        * alive
    ).astype(jnp.bfloat16)
    picked = pre_grad[places].reshape(len(live), slot_count, channels)
    returned = jnp.stack(
        [
            lax.ppermute(
                picked[place],
                "region",
                [(b, a) for a, b in neighbour_pairs(regions, DIRECTIONS[j])],
            )
            for place, j in enumerate(live)
        ]
    )
    total, input_grad = backward_conv(
        pre_grad, returned, kept, weight, from_all, to_all, live, slot_count
    )
    rounds = reduction_rounds()
    for group in rounds:
        total = sum_share(total, sent_shares(total, group), group)
    own = total.astype(jnp.bfloat16)
    for group in reversed(rounds[1:]):
        own = gathered_shares(own, group)
    place, ((_, permutation),) = place_in(rounds[0])
    other = lax.ppermute(own, ("region", "dp"), permutation)
    weight_grad = unpack_matrices(own, other, place, weight.shape[0], channels)
    return (activated[None], input_grad[None], weight_grad, gain_grad, shift_grad)


def solution(mesh):
    return jax.shard_map(
        on_device,
        mesh=mesh,
        in_specs=(
            P("dp", "region", None),
            P(),
            P(),
            P(),
            P("dp", "region", None),
            P("dp", "region"),
            P("dp", "region", None, None),
            P("dp", "region", None, None),
            P("dp", "region", None, None),
        ),
        out_specs=(P("dp", "region", None), P("dp", "region", None), P(), P(), P()),
        check_vma=False,
    )
```

```python
import jax
import jax.numpy as jnp
from jax import lax
from jax.experimental import pallas as pl
from jax.experimental.pallas import tpu as pltpu
from jax.sharding import PartitionSpec as P

GRID_W = 8
DIRECTIONS = ((-1, -1), (-1, 0), (-1, 1), (0, -1), (0, 1), (1, -1), (1, 0), (1, 1))
EPSILON = 1e-05
LANES = 128
CHAINS = 8
SCATTER_UNROLL = 16
HALF_ROWS = 4096
LAND_UNROLL = 16
UNPACK = 7
VMEM_LIMIT = 60 << 20


def live_directions(regions):
    rows = regions // GRID_W
    return [j for j, (dr, dc) in enumerate(DIRECTIONS) if abs(dr) < rows and abs(dc) < GRID_W]


def neighbour_pairs(regions, step):
    rows = regions // GRID_W
    pairs = []
    for r in range(regions):
        row, col = r // GRID_W + step[0], r % GRID_W + step[1]
        if 0 <= row < rows and 0 <= col < GRID_W:
            pairs.append((r, row * GRID_W + col))
    return pairs


def fill_table(table, first, rows):
    count, channels = rows.shape
    rows = rows.astype(jnp.float32)
    table[pl.ds(2 * first, count, stride=2), :] = rows[:, :LANES]
    rest = jnp.concatenate(
        [rows[:, LANES:], jnp.zeros((count, 2 * LANES - channels), jnp.float32)], axis=1
    )
    table[pl.ds(2 * first + 1, count, stride=2), :] = rest


def gather_and_scatter(gather_index, table, gbuf, scatter_index, vbuf, sums, pairs):
    per_chain = pairs // CHAINS

    @pl.loop(0, per_chain, step=SCATTER_UNROLL)
    def _(start):
        for u in range(SCATTER_UNROLL):
            for chain in range(CHAINS):
                pair = chain * per_chain + start + u
                place = pl.multiple_of(pair * 2, 2)
                target = pl.multiple_of(scatter_index[0, 0, pair], 2)
                sums[chain][pl.ds(target, 2), :] += vbuf[pl.ds(place, 2), :]
                source = pl.multiple_of(gather_index[0, 0, pair], 2)
                gbuf[pl.ds(place, 2), :] = table[pl.ds(source, 2), :]


def joined(buffer, pairs, channels):
    low = buffer[pl.ds(0, pairs, stride=2), :]
    high = buffer[pl.ds(1, pairs, stride=2), :]
    return jnp.concatenate([low, high[:, : channels - LANES]], axis=1)


def chain_total(sums, first, count, channels):
    low = sums[0][pl.ds(2 * first, count, stride=2), :]
    high = sums[0][pl.ds(2 * first + 1, count, stride=2), :]
    for part in sums[1:]:
        low += part[pl.ds(2 * first, count, stride=2), :]
        high += part[pl.ds(2 * first + 1, count, stride=2), :]
    return jnp.concatenate([low, high[:, : channels - LANES]], axis=1)


def round_up(n, m):
    return (n + m - 1) // m * m


def packed_rows(channels):
    return channels + channels // 2


def doubling_steps():
    steps = []
    for axis in ("dp", "region"):
        stride = 1
        while stride < lax.axis_size(axis):
            steps.append((stride, axis))
            stride *= 2
    return [(axis, stride) for stride, axis in sorted(steps)]


def exchange(value, axis, stride):
    return lax.ppermute(value, axis, [(i, i ^ stride) for i in range(lax.axis_size(axis))])


def all_sum(value):
    for axis, stride in doubling_steps():
        value = value + exchange(value, axis, stride)
    return value


def all_moments(value):
    for axis, stride in doubling_steps():
        other = exchange(value, axis, stride)
        total = value[0] + other[0]
        gap = other[1] - value[1]
        value = jnp.stack(
            [
                total,
                (value[0] * value[1] + other[0] * other[1]) / total,
                value[2] + other[2] + gap * gap * (value[0] * other[0] / total),
            ]
        )
    return value[0], value[1], value[2]


def reduction_rounds():
    steps = doubling_steps()
    return [steps[:1]] + [steps[i : i + 2] for i in range(1, len(steps), 2)]


def place_in(group):
    place = 0
    for bit, (axis, stride) in enumerate(group):
        place = place + (lax.axis_index(axis) // stride) % 2 * (1 << bit)
    inner = lax.axis_size("dp")
    count = inner * lax.axis_size("region")
    permutations = []
    for mask in range(1, 1 << len(group)):
        flip = 0
        for bit, (axis, stride) in enumerate(group):
            if mask >> bit & 1:
                flip ^= stride * (inner if axis == "region" else 1)
        permutations.append((mask, [(i, i ^ flip) for i in range(count)]))
    return place, permutations


def sent_shares(value, group):
    place, permutations = place_in(group)
    share = value.shape[0] >> len(group)
    return [
        lax.dynamic_slice_in_dim(value, (place ^ mask) * share, share, 0).astype(jnp.bfloat16)
        for mask, _ in permutations
    ]


def sum_share(value, sent, group):
    place, permutations = place_in(group)
    share = value.shape[0] >> len(group)
    total = lax.dynamic_slice_in_dim(value, place * share, share, 0).astype(jnp.float32)
    for part, (_, permutation) in zip(sent, permutations):
        got = lax.ppermute(part, ("region", "dp"), permutation)
        total = total + got.astype(jnp.float32)
    return total


def gathered_shares(value, group):
    place, permutations = place_in(group)
    shares = [value] + [
        lax.ppermute(value, ("region", "dp"), permutation) for _, permutation in permutations
    ]
    ordered = []
    for position in range(len(shares)):
        chosen = shares[position]
        for own in range(1, len(shares)):
            chosen = jnp.where(place == own, shares[own ^ position], chosen)
        ordered.append(chosen)
    return jnp.concatenate(ordered, axis=0)


def unpack_half(packed, which, offsets, channels, before=None):
    height = packed_rows(channels)
    rest = channels - LANES
    steps = round_up(offsets, 2) // 2 // UNPACK

    def kernel(which_ref, in_ref, *refs):
        out_ref = refs[-1]
        for position in range(UNPACK):
            value = in_ref[position * height : (position + 1) * height].astype(jnp.float32)
            out_ref[position, :, :LANES] = value[:channels]
            out_ref[position, : channels // 2, LANES:] = value[channels:, :rest]
            out_ref[position, channels // 2 :, LANES:] = value[channels:, rest:]

    extra = [] if before is None else [before]
    return pl.pallas_call(
        kernel,
        grid_spec=pltpu.PrefetchScalarGridSpec(
            num_scalar_prefetch=1,
            grid=(steps,),
            in_specs=[pl.BlockSpec((UNPACK * height, LANES), lambda k, which: (k, 0))]
            + [pl.BlockSpec(memory_space=pl.ANY)] * len(extra),
            out_specs=pl.BlockSpec(
                (UNPACK, channels, channels), lambda k, which: (which[0] * steps + k, 0, 0)
            ),
        ),
        out_shape=jax.ShapeDtypeStruct((offsets, channels, channels), jnp.float32),
        input_output_aliases={} if before is None else {2: 0},
        name="unpack_half",
    )(which.reshape(1).astype(jnp.int32), packed, *extra)


def forward_conv(features, weight, sources, targets, live, slots):
    rows, channels = features.shape
    offsets, _, pairs = sources.shape
    extended = round_up(rows + 8 * slots + 1, 8)
    ndir = len(live)

    def kernel(src_ref, dst_ref, x_ref, w_ref, summed_ref, out_ref, kept_ref, table, gbuf, vbuf, *sums):
        k = pl.program_id(0)

        @pl.when(k == 0)
        def _():
            fill_table(table, 0, x_ref[...])
            vbuf[...] = jnp.zeros_like(vbuf)
            for part in sums:
                part[...] = jnp.zeros_like(part)

        gather_and_scatter(src_ref, table, gbuf, dst_ref, vbuf, sums, pairs)
        picked = joined(gbuf, pairs, channels).astype(jnp.bfloat16)
        kept_ref[0] = picked
        product = jnp.dot(picked, w_ref[0], preferred_element_type=jnp.float32)
        fill_table(vbuf, 0, product)

        @pl.when(k == offsets)
        def _():
            for first in range(0, rows, 256):
                summed_ref[pl.ds(first, 256), :] = chain_total(sums, first, 256, channels)
            for place, j in enumerate(live):
                out_ref[place] = chain_total(sums, rows + j * slots, slots, channels).astype(
                    jnp.bfloat16
                )

    now = lambda k: (jnp.minimum(k, offsets - 1), 0, 0)
    before = lambda k: (jnp.maximum(k - 1, 0), 0, 0)
    smem = lambda where: pl.BlockSpec((1, 1, pairs), where, memory_space=pltpu.SMEM)
    return pl.pallas_call(
        kernel,
        grid=(offsets + 1,),
        in_specs=[
            smem(now),
            smem(before),
            pl.BlockSpec((rows, channels), lambda k: (0, 0)),
            pl.BlockSpec((1, channels, channels), now),
        ],
        out_specs=[
            pl.BlockSpec((rows, channels), lambda k: (0, 0)),
            pl.BlockSpec((ndir, slots, channels), lambda k: (0, 0, 0)),
            pl.BlockSpec((1, pairs, channels), now),
        ],
        out_shape=[
            jax.ShapeDtypeStruct((rows, channels), jnp.float32),
            jax.ShapeDtypeStruct((ndir, slots, channels), jnp.bfloat16),
            jax.ShapeDtypeStruct((offsets, pairs, channels), jnp.bfloat16),
        ],
        scratch_shapes=[
            pltpu.VMEM((2 * rows, LANES), jnp.float32),
            pltpu.VMEM((2 * pairs, LANES), jnp.float32),
            pltpu.VMEM((2 * pairs, LANES), jnp.float32),
        ]
        + [pltpu.VMEM((2 * extended, LANES), jnp.float32)] * CHAINS,
        compiler_params=pltpu.CompilerParams(vmem_limit_bytes=VMEM_LIMIT),
        name="forward_conv",
    )(sources, targets, features, weight)


def landed_moments(summed, arrivals, places, count):
    rows, channels = summed.shape
    slots = arrivals[0].shape[0]
    total = slots * len(arrivals)

    def kernel(place_ref, count_ref, summed_ref, *refs):
        arrived = refs[: len(arrivals)]
        preact_ref, moments_ref, incoming = refs[len(arrivals) :]
        preact_ref[...] = summed_ref[...]
        for number, part in enumerate(arrived):
            incoming[number * slots : (number + 1) * slots, :] = part[...].astype(jnp.float32)

        @pl.loop(0, total, step=LAND_UNROLL)
        def _(start):
            for u in range(LAND_UNROLL):
                preact_ref[pl.ds(place_ref[start + u], 1), :] += incoming[pl.ds(start + u, 1), :]

        own = count_ref[0]
        own_float = own.astype(jnp.float32)
        block = 256

        def blocks(value):
            result = jnp.zeros((1, channels), jnp.float32)
            for first in range(0, rows, block):
                ids = first + lax.broadcasted_iota(jnp.int32, (block, 1), 0)
                part = value(preact_ref[first : first + block, :])
                result += jnp.sum(jnp.where(ids < own, part, 0.0), axis=0, keepdims=True)
            return result

        mean = blocks(lambda x: x) / own_float
        moments_ref[0:1, :] = jnp.full((1, channels), own_float)
        moments_ref[1:2, :] = mean
        moments_ref[2:3, :] = blocks(lambda x: (x - mean) * (x - mean))

    smem = pl.BlockSpec(memory_space=pltpu.SMEM)
    vmem = pl.BlockSpec(memory_space=pltpu.VMEM)
    return pl.pallas_call(
        kernel,
        in_specs=[smem, smem] + [vmem] * (1 + len(arrivals)),
        out_specs=[vmem, vmem],
        out_shape=[
            jax.ShapeDtypeStruct((rows, channels), jnp.float32),
            jax.ShapeDtypeStruct((3, channels), jnp.float32),
        ],
        scratch_shapes=[pltpu.VMEM((total, channels), jnp.float32)],
        compiler_params=pltpu.CompilerParams(vmem_limit_bytes=32 << 20),
        name="landed_moments",
    )(places, count, summed, *arrivals)


def backward_conv(pre_grad, returned, kept, weight, sources, targets, live, slots):
    rows, channels = pre_grad.shape
    offsets, _, pairs = sources.shape
    extended = round_up(rows + 8 * slots + 1, 8)
    ndir = len(live)
    height = packed_rows(channels)
    half = round_up(offsets, 2) // 2
    half_rows = round_up(half * height, HALF_ROWS)

    def kernel(src_ref, dst_ref, g_ref, ret_ref, x_ref, w_ref, wgrad_ref, xgrad_ref, table, gbuf, vbuf, *sums):
        k = pl.program_id(0)

        @pl.when(k == 0)
        def _():
            fill_table(table, 0, g_ref[...])
            for place, j in enumerate(live):
                fill_table(table, rows + j * slots, ret_ref[place])
            tail = 2 * (rows + 8 * slots)
            table[tail:, :] = jnp.zeros((2 * extended - tail, LANES), jnp.float32)
            vbuf[...] = jnp.zeros_like(vbuf)
            wgrad_ref[half * height : half_rows, :] = jnp.zeros(
                (half_rows - half * height, LANES), jnp.bfloat16
            )
            used = half_rows + (offsets - half) * height
            wgrad_ref[used:, :] = jnp.zeros((2 * half_rows - used, LANES), jnp.bfloat16)
            for part in sums:
                part[...] = jnp.zeros_like(part)

        gather_and_scatter(dst_ref, table, gbuf, src_ref, vbuf, sums, pairs)
        picked = joined(gbuf, pairs, channels).astype(jnp.bfloat16)
        wgrad = lax.dot_general(
            x_ref[0], picked, (((0,), (0,)), ((), ())), preferred_element_type=jnp.float32
        ).astype(jnp.bfloat16)
        at = jnp.minimum(k, offsets - 1)
        first = jnp.where(at < half, at * height, half_rows + (at - half) * height)
        first = pl.multiple_of(first, 32)
        wgrad_ref[pl.ds(first, channels), :] = wgrad[:, :LANES]
        wgrad_ref[pl.ds(first + channels, channels // 2), :] = jnp.concatenate(
            [wgrad[: channels // 2, LANES:], wgrad[channels // 2 :, LANES:]], axis=1
        )
        product = lax.dot_general(
            picked, w_ref[0], (((1,), (1,)), ((), ())), preferred_element_type=jnp.float32
        )
        fill_table(vbuf, 0, product)

        @pl.when(k == offsets)
        def _():
            for first in range(0, rows, 256):
                xgrad_ref[pl.ds(first, 256), :] = chain_total(sums, first, 256, channels).astype(
                    jnp.bfloat16
                )

    now = lambda k: (jnp.minimum(k, offsets - 1), 0, 0)
    before = lambda k: (jnp.maximum(k - 1, 0), 0, 0)
    smem = lambda where: pl.BlockSpec((1, 1, pairs), where, memory_space=pltpu.SMEM)
    return pl.pallas_call(
        kernel,
        grid=(offsets + 1,),
        in_specs=[
            smem(before),
            smem(now),
            pl.BlockSpec((rows, channels), lambda k: (0, 0)),
            pl.BlockSpec((ndir, slots, channels), lambda k: (0, 0, 0)),
            pl.BlockSpec((1, pairs, channels), now),
            pl.BlockSpec((1, channels, channels), now),
        ],
        out_specs=[
            pl.BlockSpec((2 * half_rows, LANES), lambda k: (0, 0)),
            pl.BlockSpec((rows, channels), lambda k: (0, 0)),
        ],
        out_shape=[
            jax.ShapeDtypeStruct((2 * half_rows, LANES), jnp.bfloat16),
            jax.ShapeDtypeStruct((rows, channels), jnp.bfloat16),
        ],
        scratch_shapes=[
            pltpu.VMEM((2 * extended, LANES), jnp.float32),
            pltpu.VMEM((2 * pairs, LANES), jnp.float32),
            pltpu.VMEM((2 * pairs, LANES), jnp.float32),
        ]
        + [pltpu.VMEM((2 * rows, LANES), jnp.float32)] * CHAINS,
        compiler_params=pltpu.CompilerParams(vmem_limit_bytes=VMEM_LIMIT),
        name="backward_conv",
    )(sources, targets, pre_grad, returned, kept, weight)


def on_device(
    features, weight, norm_gain, norm_shift, cotangent, counts, in_rows, out_slots, land_rows
):
    regions = lax.axis_size("region")
    live = live_directions(regions)
    voxels = features[0]
    row_count, channels = voxels.shape
    from_all = (in_rows[0, 0] * 2)[:, None, :]
    to_all = (out_slots[0, 0] * 2)[:, None, :]
    slot_count = land_rows.shape[3]
    places = jnp.concatenate([land_rows[0, 0, j] for j in live])
    summed, outgoing, kept = forward_conv(voxels, weight, from_all, to_all, live, slot_count)
    arrivals = [
        lax.ppermute(outgoing[place], "region", neighbour_pairs(regions, DIRECTIONS[j]))
        for place, j in enumerate(live)
    ]
    preact, moments = landed_moments(summed, arrivals, places, counts[0])
    alive = (lax.broadcasted_iota(jnp.int32, (row_count, 1), 0) < counts[0, 0]).astype(jnp.float32)
    count_total, average, square = all_moments(moments)
    variance = square / count_total
    inverse = lax.rsqrt(variance + EPSILON)
    normed = (preact - average) * inverse
    shifted = norm_gain * normed + norm_shift
    sigma = jax.nn.sigmoid(shifted)
    slope = sigma * (1.0 + shifted * (1.0 - sigma)) * alive
    activated = (shifted * sigma * alive).astype(jnp.bfloat16)
    upstream = cotangent[0].astype(jnp.float32) * slope
    gain_grad, shift_grad = all_sum(
        jnp.stack([jnp.sum(upstream * normed, axis=0), jnp.sum(upstream, axis=0)])
    )
    pre_grad = (
        norm_gain
        * inverse
        * (upstream - shift_grad / count_total - normed * gain_grad / count_total)
        * alive
    ).astype(jnp.bfloat16)
    picked = pre_grad[places].reshape(len(live), slot_count, channels)
    returned = jnp.stack(
        [
            lax.ppermute(
                picked[place],
                "region",
                [(b, a) for a, b in neighbour_pairs(regions, DIRECTIONS[j])],
            )
            for place, j in enumerate(live)
        ]
    )
    total, input_grad = backward_conv(
        pre_grad, returned, kept, weight, from_all, to_all, live, slot_count
    )
    rounds = reduction_rounds()
    for group in rounds:
        total = sum_share(total, sent_shares(total, group), group)
    own = total.astype(jnp.bfloat16)
    for group in reversed(rounds[1:]):
        own = gathered_shares(own, group)
    place, ((_, permutation),) = place_in(rounds[0])
    other = lax.ppermute(own, ("region", "dp"), permutation)
    weight_grad = unpack_half(own, place, weight.shape[0], channels)
    weight_grad = unpack_half(other, 1 - place, weight.shape[0], channels, weight_grad)
    return (activated[None], input_grad[None], weight_grad, gain_grad, shift_grad)


def solution(mesh):
    return jax.shard_map(
        on_device,
        mesh=mesh,
        in_specs=(
            P("dp", "region", None),
            P(),
            P(),
            P(),
            P("dp", "region", None),
            P("dp", "region"),
            P("dp", "region", None, None),
            P("dp", "region", None, None),
            P("dp", "region", None, None),
        ),
        out_specs=(P("dp", "region", None), P("dp", "region", None), P(), P(), P()),
        check_vma=False,
    )
```

```python
import jax
import jax.numpy as jnp
from jax import lax
from jax.experimental import pallas as pl
from jax.experimental.pallas import tpu as pltpu
from jax.sharding import PartitionSpec as P

GRID_W = 8
DIRECTIONS = ((-1, -1), (-1, 0), (-1, 1), (0, -1), (0, 1), (1, -1), (1, 0), (1, 1))
EPSILON = 1e-05
LANES = 128
CHAINS = 8
SCATTER_UNROLL = 32
HALF_ROWS = 4096
LAND_UNROLL = 16
UNPACK = 7
VMEM_LIMIT = 60 << 20


def live_directions(regions):
    rows = regions // GRID_W
    return [j for j, (dr, dc) in enumerate(DIRECTIONS) if abs(dr) < rows and abs(dc) < GRID_W]


def neighbour_pairs(regions, step):
    rows = regions // GRID_W
    pairs = []
    for r in range(regions):
        row, col = r // GRID_W + step[0], r % GRID_W + step[1]
        if 0 <= row < rows and 0 <= col < GRID_W:
            pairs.append((r, row * GRID_W + col))
    return pairs


def fill_table(table, first, rows):
    count, channels = rows.shape
    rows = rows.astype(jnp.float32)
    table[pl.ds(2 * first, count, stride=2), :] = rows[:, :LANES]
    rest = jnp.concatenate(
        [rows[:, LANES:], jnp.zeros((count, 2 * LANES - channels), jnp.float32)], axis=1
    )
    table[pl.ds(2 * first + 1, count, stride=2), :] = rest


def gather_and_scatter(gather_index, table, gbuf, scatter_index, vbuf, sums, pairs):
    per_chain = pairs // CHAINS

    @pl.loop(0, per_chain, step=SCATTER_UNROLL)
    def _(start):
        for u in range(SCATTER_UNROLL):
            for chain in range(CHAINS):
                pair = chain * per_chain + start + u
                place = pl.multiple_of(pair * 2, 2)
                target = pl.multiple_of(scatter_index[0, 0, pair], 2)
                sums[chain][pl.ds(target, 2), :] += vbuf[pl.ds(place, 2), :]
                source = pl.multiple_of(gather_index[0, 0, pair], 2)
                gbuf[pl.ds(place, 2), :] = table[pl.ds(source, 2), :]


def joined(buffer, pairs):
    low = buffer[pl.ds(0, pairs, stride=2), :].astype(jnp.bfloat16)
    high = buffer[pl.ds(1, pairs, stride=2), :].astype(jnp.bfloat16)
    return jnp.concatenate([low, high], axis=1)


def chain_total(sums, first, count, channels):
    low = sums[0][pl.ds(2 * first, count, stride=2), :]
    high = sums[0][pl.ds(2 * first + 1, count, stride=2), :]
    for part in sums[1:]:
        low += part[pl.ds(2 * first, count, stride=2), :]
        high += part[pl.ds(2 * first + 1, count, stride=2), :]
    return jnp.concatenate([low, high[:, : channels - LANES]], axis=1)


def round_up(n, m):
    return (n + m - 1) // m * m


def packed_rows(channels):
    return channels + channels // 2


def doubling_steps():
    steps = []
    for axis in ("dp", "region"):
        stride = 1
        while stride < lax.axis_size(axis):
            steps.append((stride, axis))
            stride *= 2
    return [(axis, stride) for stride, axis in sorted(steps)]


def exchange(value, axis, stride):
    return lax.ppermute(value, axis, [(i, i ^ stride) for i in range(lax.axis_size(axis))])


def from_all(value):
    count = lax.axis_size("region") * lax.axis_size("dp")
    flat = jnp.broadcast_to(value.reshape(1, 1, -1), (count, 1, value.size))
    flat = lax.all_to_all(flat, ("region", "dp"), 0, 0, tiled=True)
    return flat.reshape((count,) + value.shape)


def all_sum(value):
    return jnp.sum(from_all(value), axis=0)


def all_moments(value):
    value = from_all(value)
    count, mean, square = value[:, 0], value[:, 1], value[:, 2]
    total = jnp.sum(count, axis=0)
    average = jnp.sum(count * mean, axis=0) / total
    gap = mean - average
    return total, average, jnp.sum(square + count * gap * gap, axis=0)


def reduction_rounds():
    steps = doubling_steps()
    return [steps[:1]] + [steps[i : i + 2] for i in range(1, len(steps), 2)]


def place_in(group):
    place = 0
    for bit, (axis, stride) in enumerate(group):
        place = place + (lax.axis_index(axis) // stride) % 2 * (1 << bit)
    inner = lax.axis_size("dp")
    count = inner * lax.axis_size("region")
    permutations = []
    for mask in range(1, 1 << len(group)):
        flip = 0
        for bit, (axis, stride) in enumerate(group):
            if mask >> bit & 1:
                flip ^= stride * (inner if axis == "region" else 1)
        permutations.append((mask, [(i, i ^ flip) for i in range(count)]))
    return place, permutations


def sent_shares(value, group):
    place, permutations = place_in(group)
    share = value.shape[0] >> len(group)
    return [
        lax.dynamic_slice_in_dim(value, (place ^ mask) * share, share, 0).astype(jnp.bfloat16)
        for mask, _ in permutations
    ]


def sum_share(value, sent, group):
    place, permutations = place_in(group)
    share = value.shape[0] >> len(group)
    total = lax.dynamic_slice_in_dim(value, place * share, share, 0).astype(jnp.float32)
    for part, (_, permutation) in zip(sent, permutations):
        got = lax.ppermute(part, ("region", "dp"), permutation)
        total = total + got.astype(jnp.float32)
    return total


def gathered_shares(value, group):
    place, permutations = place_in(group)
    shares = [value] + [
        lax.ppermute(value, ("region", "dp"), permutation) for _, permutation in permutations
    ]
    ordered = []
    for position in range(len(shares)):
        chosen = shares[position]
        for own in range(1, len(shares)):
            chosen = jnp.where(place == own, shares[own ^ position], chosen)
        ordered.append(chosen)
    return jnp.concatenate(ordered, axis=0)


def unpack_half(packed, which, offsets, channels, before=None):
    height = packed_rows(channels)
    rest = channels - LANES
    steps = round_up(offsets, 2) // 2 // UNPACK

    def kernel(which_ref, in_ref, *refs):
        out_ref = refs[-1]
        for position in range(UNPACK):
            value = in_ref[position * height : (position + 1) * height].astype(jnp.float32)
            out_ref[position, :, :LANES] = value[:channels]
            out_ref[position, : channels // 2, LANES:] = value[channels:, :rest]
            out_ref[position, channels // 2 :, LANES:] = value[channels:, rest:]

    extra = [] if before is None else [before]
    return pl.pallas_call(
        kernel,
        grid_spec=pltpu.PrefetchScalarGridSpec(
            num_scalar_prefetch=1,
            grid=(steps,),
            in_specs=[pl.BlockSpec((UNPACK * height, LANES), lambda k, which: (k, 0))]
            + [pl.BlockSpec(memory_space=pl.ANY)] * len(extra),
            out_specs=pl.BlockSpec(
                (UNPACK, channels, channels), lambda k, which: (which[0] * steps + k, 0, 0)
            ),
        ),
        out_shape=jax.ShapeDtypeStruct((offsets, channels, channels), jnp.float32),
        input_output_aliases={} if before is None else {2: 0},
        name="unpack_half",
    )(which.reshape(1).astype(jnp.int32), packed, *extra)


def forward_conv(features, weight, sources, targets, live, slots):
    rows, channels = features.shape
    offsets, _, pairs = sources.shape
    extended = round_up(rows + 8 * slots + 1, 8)
    ndir = len(live)

    def kernel(src_ref, dst_ref, x_ref, w_ref, summed_ref, kept_ref, *refs):
        out_refs = refs[:ndir]
        table, gbuf, vbuf, *sums = refs[ndir:]
        k = pl.program_id(0)

        @pl.when(k == 0)
        def _():
            fill_table(table, 0, x_ref[...])
            vbuf[...] = jnp.zeros_like(vbuf)
            for part in sums:
                part[: 2 * rows, :] = jnp.zeros((2 * rows, LANES), jnp.float32)
                for j in live:
                    part[pl.ds(2 * (rows + j * slots), 2 * slots), :] = jnp.zeros(
                        (2 * slots, LANES), jnp.float32
                    )

        gather_and_scatter(src_ref, table, gbuf, dst_ref, vbuf, sums, pairs)
        picked = joined(gbuf, pairs)
        kept_ref[0] = picked
        product = jnp.dot(picked[:, :channels], w_ref[0], preferred_element_type=jnp.float32)
        fill_table(vbuf, 0, product)

        @pl.when(k == offsets)
        def _():
            for first in range(0, rows, 256):
                summed_ref[pl.ds(first, 256), :] = chain_total(sums, first, 256, channels)
            for place, j in enumerate(live):
                out_refs[place][...] = chain_total(sums, rows + j * slots, slots, channels).astype(
                    jnp.bfloat16
                )

    now = lambda k: (jnp.minimum(k, offsets - 1), 0, 0)
    before = lambda k: (jnp.maximum(k - 1, 0), 0, 0)
    smem = lambda where: pl.BlockSpec((1, 1, pairs), where, memory_space=pltpu.SMEM)
    return pl.pallas_call(
        kernel,
        grid=(offsets + 1,),
        in_specs=[
            smem(now),
            smem(before),
            pl.BlockSpec((rows, channels), lambda k: (0, 0)),
            pl.BlockSpec((1, channels, channels), now),
        ],
        out_specs=[
            pl.BlockSpec((rows, channels), lambda k: (0, 0)),
            pl.BlockSpec((1, pairs, 2 * LANES), now),
        ]
        + [pl.BlockSpec((slots, channels), lambda k: (0, 0))] * ndir,
        out_shape=[
            jax.ShapeDtypeStruct((rows, channels), jnp.float32),
            jax.ShapeDtypeStruct((offsets, pairs, 2 * LANES), jnp.bfloat16),
        ]
        + [jax.ShapeDtypeStruct((slots, channels), jnp.bfloat16)] * ndir,
        scratch_shapes=[
            pltpu.VMEM((2 * rows, LANES), jnp.float32),
            pltpu.VMEM((2 * pairs, LANES), jnp.float32),
            pltpu.VMEM((2 * pairs, LANES), jnp.float32),
        ]
        + [pltpu.VMEM((2 * extended, LANES), jnp.float32)] * CHAINS,
        compiler_params=pltpu.CompilerParams(vmem_limit_bytes=VMEM_LIMIT),
        name="forward_conv",
    )(sources, targets, features, weight)


def landed_moments(summed, arrivals, places, count):
    rows, channels = summed.shape
    slots = arrivals[0].shape[0]
    total = slots * len(arrivals)

    def kernel(place_ref, count_ref, summed_ref, *refs):
        arrived = refs[: len(arrivals)]
        preact_ref, moments_ref, incoming = refs[len(arrivals) :]
        preact_ref[...] = summed_ref[...]
        for number, part in enumerate(arrived):
            incoming[number * slots : (number + 1) * slots, :] = part[...].astype(jnp.float32)

        @pl.loop(0, total, step=LAND_UNROLL)
        def _(start):
            for u in range(LAND_UNROLL):
                preact_ref[pl.ds(place_ref[start + u], 1), :] += incoming[pl.ds(start + u, 1), :]

        own = count_ref[0]
        own_float = own.astype(jnp.float32)
        block = 256

        def blocks(value):
            result = jnp.zeros((1, channels), jnp.float32)
            for first in range(0, rows, block):
                ids = first + lax.broadcasted_iota(jnp.int32, (block, 1), 0)
                part = value(preact_ref[first : first + block, :])
                result += jnp.sum(jnp.where(ids < own, part, 0.0), axis=0, keepdims=True)
            return result

        mean = blocks(lambda x: x) / own_float
        moments_ref[0:1, :] = jnp.full((1, channels), own_float)
        moments_ref[1:2, :] = mean
        moments_ref[2:3, :] = blocks(lambda x: (x - mean) * (x - mean))

    smem = pl.BlockSpec(memory_space=pltpu.SMEM)
    vmem = pl.BlockSpec(memory_space=pltpu.VMEM)
    return pl.pallas_call(
        kernel,
        in_specs=[smem, smem] + [vmem] * (1 + len(arrivals)),
        out_specs=[vmem, vmem],
        out_shape=[
            jax.ShapeDtypeStruct((rows, channels), jnp.float32),
            jax.ShapeDtypeStruct((3, channels), jnp.float32),
        ],
        scratch_shapes=[pltpu.VMEM((total, channels), jnp.float32)],
        compiler_params=pltpu.CompilerParams(vmem_limit_bytes=32 << 20),
        name="landed_moments",
    )(places, count, summed, *arrivals)


def backward_conv(pre_grad, returned, kept, weight, sources, targets, live, slots):
    rows, channels = pre_grad.shape
    offsets, _, pairs = sources.shape
    extended = round_up(rows + 8 * slots + 1, 8)
    ndir = len(live)
    height = packed_rows(channels)
    half = round_up(offsets, 2) // 2
    half_rows = round_up(half * height, HALF_ROWS)

    def kernel(src_ref, dst_ref, g_ref, x_ref, w_ref, *refs):
        ret_refs = refs[:ndir]
        wgrad_ref, xgrad_ref, table, gbuf, vbuf, *sums = refs[ndir:]
        k = pl.program_id(0)

        @pl.when(k == 0)
        def _():
            fill_table(table, 0, g_ref[...])
            for place, j in enumerate(live):
                fill_table(table, rows + j * slots, ret_refs[place][...])
            tail = 2 * (rows + 8 * slots)
            table[tail:, :] = jnp.zeros((2 * extended - tail, LANES), jnp.float32)
            vbuf[...] = jnp.zeros_like(vbuf)
            wgrad_ref[half * height : half_rows, :] = jnp.zeros(
                (half_rows - half * height, LANES), jnp.bfloat16
            )
            used = half_rows + (offsets - half) * height
            wgrad_ref[used:, :] = jnp.zeros((2 * half_rows - used, LANES), jnp.bfloat16)
            for part in sums:
                part[...] = jnp.zeros_like(part)

        gather_and_scatter(dst_ref, table, gbuf, src_ref, vbuf, sums, pairs)
        picked = joined(gbuf, pairs)[:, :channels]
        wgrad = lax.dot_general(
            x_ref[0, :, :channels], picked, (((0,), (0,)), ((), ())), preferred_element_type=jnp.float32
        ).astype(jnp.bfloat16)
        at = jnp.minimum(k, offsets - 1)
        first = jnp.where(at < half, at * height, half_rows + (at - half) * height)
        first = pl.multiple_of(first, 32)
        wgrad_ref[pl.ds(first, channels), :] = wgrad[:, :LANES]
        wgrad_ref[pl.ds(first + channels, channels // 2), :] = jnp.concatenate(
            [wgrad[: channels // 2, LANES:], wgrad[channels // 2 :, LANES:]], axis=1
        )
        product = lax.dot_general(
            picked, w_ref[0], (((1,), (1,)), ((), ())), preferred_element_type=jnp.float32
        )
        fill_table(vbuf, 0, product)

        @pl.when(k == offsets)
        def _():
            for first in range(0, rows, 256):
                xgrad_ref[pl.ds(first, 256), :] = chain_total(sums, first, 256, channels).astype(
                    jnp.bfloat16
                )

    now = lambda k: (jnp.minimum(k, offsets - 1), 0, 0)
    before = lambda k: (jnp.maximum(k - 1, 0), 0, 0)
    smem = lambda where: pl.BlockSpec((1, 1, pairs), where, memory_space=pltpu.SMEM)
    return pl.pallas_call(
        kernel,
        grid=(offsets + 1,),
        in_specs=[
            smem(before),
            smem(now),
            pl.BlockSpec((rows, channels), lambda k: (0, 0)),
            pl.BlockSpec((1, pairs, 2 * LANES), now),
            pl.BlockSpec((1, channels, channels), now),
        ]
        + [pl.BlockSpec((slots, channels), lambda k: (0, 0))] * ndir,
        out_specs=[
            pl.BlockSpec((2 * half_rows, LANES), lambda k: (0, 0)),
            pl.BlockSpec((rows, channels), lambda k: (0, 0)),
        ],
        out_shape=[
            jax.ShapeDtypeStruct((2 * half_rows, LANES), jnp.bfloat16),
            jax.ShapeDtypeStruct((rows, channels), jnp.bfloat16),
        ],
        scratch_shapes=[
            pltpu.VMEM((2 * extended, LANES), jnp.float32),
            pltpu.VMEM((2 * pairs, LANES), jnp.float32),
            pltpu.VMEM((2 * pairs, LANES), jnp.float32),
        ]
        + [pltpu.VMEM((2 * rows, LANES), jnp.float32)] * CHAINS,
        compiler_params=pltpu.CompilerParams(vmem_limit_bytes=VMEM_LIMIT),
        name="backward_conv",
    )(sources, targets, pre_grad, kept, weight, *returned)


def on_device(
    features, weight, norm_gain, norm_shift, cotangent, counts, in_rows, out_slots, land_rows
):
    regions = lax.axis_size("region")
    live = live_directions(regions)
    voxels = features[0]
    row_count, channels = voxels.shape
    sources = (in_rows[0, 0] * 2)[:, None, :]
    targets = (out_slots[0, 0] * 2)[:, None, :]
    slot_count = land_rows.shape[3]
    places = jnp.concatenate([land_rows[0, 0, j] for j in live])
    summed, kept, *outgoing = forward_conv(voxels, weight, sources, targets, live, slot_count)
    arrivals = [
        lax.ppermute(outgoing[place], "region", neighbour_pairs(regions, DIRECTIONS[j]))
        for place, j in enumerate(live)
    ]
    preact, moments = landed_moments(summed, arrivals, places, counts[0])
    alive = (lax.broadcasted_iota(jnp.int32, (row_count, 1), 0) < counts[0, 0]).astype(jnp.float32)
    count_total, average, square = all_moments(moments)
    variance = square / count_total
    inverse = lax.rsqrt(variance + EPSILON)
    normed = (preact - average) * inverse
    shifted = norm_gain * normed + norm_shift
    sigma = jax.nn.sigmoid(shifted)
    slope = sigma * (1.0 + shifted * (1.0 - sigma)) * alive
    activated = (shifted * sigma * alive).astype(jnp.bfloat16)
    upstream = cotangent[0].astype(jnp.float32) * slope
    gain_grad, shift_grad = all_sum(
        jnp.stack([jnp.sum(upstream * normed, axis=0), jnp.sum(upstream, axis=0)])
    )
    pre_grad = (
        norm_gain
        * inverse
        * (upstream - shift_grad / count_total - normed * gain_grad / count_total)
        * alive
    ).astype(jnp.bfloat16)
    picked = pre_grad[places].reshape(len(live), slot_count, channels)
    returned = [
        lax.ppermute(
            picked[place], "region", [(b, a) for a, b in neighbour_pairs(regions, DIRECTIONS[j])]
        )
        for place, j in enumerate(live)
    ]
    total, input_grad = backward_conv(
        pre_grad, returned, kept, weight, sources, targets, live, slot_count
    )
    rounds = reduction_rounds()
    for group in rounds:
        total = sum_share(total, sent_shares(total, group), group)
    own = total.astype(jnp.bfloat16)
    for group in reversed(rounds[1:]):
        own = gathered_shares(own, group)
    place, ((_, permutation),) = place_in(rounds[0])
    other = lax.ppermute(own, ("region", "dp"), permutation)
    weight_grad = unpack_half(own, place, weight.shape[0], channels)
    weight_grad = unpack_half(other, 1 - place, weight.shape[0], channels, weight_grad)
    return (activated[None], input_grad[None], weight_grad, gain_grad, shift_grad)


def solution(mesh):
    return jax.shard_map(
        on_device,
        mesh=mesh,
        in_specs=(
            P("dp", "region", None),
            P(),
            P(),
            P(),
            P("dp", "region", None),
            P("dp", "region"),
            P("dp", "region", None, None),
            P("dp", "region", None, None),
            P("dp", "region", None, None),
        ),
        out_specs=(P("dp", "region", None), P("dp", "region", None), P(), P(), P()),
        check_vma=False,
    )
```

```python
import jax
import jax.numpy as jnp
from jax import lax
from jax.experimental import pallas as pl
from jax.experimental.pallas import tpu as pltpu
from jax.sharding import PartitionSpec as P

GRID_W = 8
DIRECTIONS = ((-1, -1), (-1, 0), (-1, 1), (0, -1), (0, 1), (1, -1), (1, 0), (1, 1))
EPSILON = 1e-05
LANES = 128
CHAINS = 8
SCATTER_UNROLL = 32
HALF_ROWS = 4096
LAND_UNROLL = 16
GATHER_UNROLL = 256
COVER_SUM = {1: 5}
COVER_SHARE = {1: 5}
COST_FLOPS = 2 << 30
UNPACK = 7
VMEM_LIMIT = 60 << 20


def live_directions(regions):
    rows = regions // GRID_W
    return [j for j, (dr, dc) in enumerate(DIRECTIONS) if abs(dr) < rows and abs(dc) < GRID_W]


def neighbour_pairs(regions, step):
    rows = regions // GRID_W
    pairs = []
    for r in range(regions):
        row, col = r // GRID_W + step[0], r % GRID_W + step[1]
        if 0 <= row < rows and 0 <= col < GRID_W:
            pairs.append((r, row * GRID_W + col))
    return pairs


def fill_table(table, first, rows):
    count, channels = rows.shape
    rows = rows.astype(jnp.float32)
    table[pl.ds(2 * first, count, stride=2), :] = rows[:, :LANES]
    rest = jnp.concatenate(
        [rows[:, LANES:], jnp.zeros((count, 2 * LANES - channels), jnp.float32)], axis=1
    )
    table[pl.ds(2 * first + 1, count, stride=2), :] = rest


def gather_rows(index, table, buffer, pairs):
    @pl.loop(0, pairs, step=GATHER_UNROLL)
    def _(start):
        for u in range(GATHER_UNROLL):
            source = pl.multiple_of(index[0, 0, start + u], 2)
            target = pl.multiple_of((start + u) * 2, 2)
            buffer[pl.ds(target, 2), :] = table[pl.ds(source, 2), :]


def scatter_rows(index, buffer, sums, pairs):
    per_chain = pairs // CHAINS

    @pl.loop(0, per_chain, step=SCATTER_UNROLL)
    def _(start):
        for u in range(SCATTER_UNROLL):
            for chain in range(CHAINS):
                pair = chain * per_chain + start + u
                target = pl.multiple_of(index[0, 0, pair], 2)
                source = pl.multiple_of(pair * 2, 2)
                sums[chain][pl.ds(target, 2), :] += buffer[pl.ds(source, 2), :]


def gather_and_scatter(gather_index, table, gbuf, scatter_index, vbuf, sums, pairs):
    per_chain = pairs // CHAINS

    @pl.loop(0, per_chain, step=SCATTER_UNROLL)
    def _(start):
        for u in range(SCATTER_UNROLL):
            for chain in range(CHAINS):
                pair = chain * per_chain + start + u
                place = pl.multiple_of(pair * 2, 2)
                target = pl.multiple_of(scatter_index[0, 0, pair], 2)
                sums[chain][pl.ds(target, 2), :] += vbuf[pl.ds(place, 2), :]
                source = pl.multiple_of(gather_index[0, 0, pair], 2)
                gbuf[pl.ds(place, 2), :] = table[pl.ds(source, 2), :]


def joined(buffer, pairs):
    low = buffer[pl.ds(0, pairs, stride=2), :].astype(jnp.bfloat16)
    high = buffer[pl.ds(1, pairs, stride=2), :].astype(jnp.bfloat16)
    return jnp.concatenate([low, high], axis=1)


def chain_total(sums, first, count, channels):
    low = sums[0][pl.ds(2 * first, count, stride=2), :]
    high = sums[0][pl.ds(2 * first + 1, count, stride=2), :]
    for part in sums[1:]:
        low += part[pl.ds(2 * first, count, stride=2), :]
        high += part[pl.ds(2 * first + 1, count, stride=2), :]
    return jnp.concatenate([low, high[:, : channels - LANES]], axis=1)


def round_up(n, m):
    return (n + m - 1) // m * m


def packed_rows(channels):
    return channels + channels // 2


def doubling_steps():
    steps = []
    for axis in ("dp", "region"):
        stride = 1
        while stride < lax.axis_size(axis):
            steps.append((stride, axis))
            stride *= 2
    return [(axis, stride) for stride, axis in sorted(steps)]


def exchange(value, axis, stride):
    return lax.ppermute(value, axis, [(i, i ^ stride) for i in range(lax.axis_size(axis))])


def from_all(value):
    count = lax.axis_size("region") * lax.axis_size("dp")
    flat = jnp.broadcast_to(value.reshape(1, 1, -1), (count, 1, value.size))
    flat = lax.all_to_all(flat, ("region", "dp"), 0, 0, tiled=True)
    return flat.reshape((count,) + value.shape)


def all_sum(value):
    return jnp.sum(from_all(value), axis=0)


def all_moments(value):
    value = from_all(value)
    count, mean, square = value[:, 0], value[:, 1], value[:, 2]
    total = jnp.sum(count, axis=0)
    average = jnp.sum(count * mean, axis=0) / total
    gap = mean - average
    return total, average, jnp.sum(square + count * gap * gap, axis=0)


def reduction_rounds():
    steps = doubling_steps()
    return [steps[:1]] + [steps[i : i + 2] for i in range(1, len(steps), 2)]


def place_in(group):
    place = 0
    for bit, (axis, stride) in enumerate(group):
        place = place + (lax.axis_index(axis) // stride) % 2 * (1 << bit)
    inner = lax.axis_size("dp")
    count = inner * lax.axis_size("region")
    permutations = []
    for mask in range(1, 1 << len(group)):
        flip = 0
        for bit, (axis, stride) in enumerate(group):
            if mask >> bit & 1:
                flip ^= stride * (inner if axis == "region" else 1)
        permutations.append((mask, [(i, i ^ flip) for i in range(count)]))
    return place, permutations


def sent_shares(value, group):
    place, permutations = place_in(group)
    share = value.shape[0] >> len(group)
    return [
        lax.dynamic_slice_in_dim(value, (place ^ mask) * share, share, 0).astype(jnp.bfloat16)
        for mask, _ in permutations
    ]


def sum_share(value, sent, group):
    place, permutations = place_in(group)
    share = value.shape[0] >> len(group)
    total = lax.dynamic_slice_in_dim(value, place * share, share, 0).astype(jnp.float32)
    for part, (_, permutation) in zip(sent, permutations):
        got = lax.ppermute(part, ("region", "dp"), permutation)
        total = total + got.astype(jnp.float32)
    return total


def gathered_shares(value, group):
    place, permutations = place_in(group)
    shares = [value] + [
        lax.ppermute(value, ("region", "dp"), permutation) for _, permutation in permutations
    ]
    ordered = []
    for position in range(len(shares)):
        chosen = shares[position]
        for own in range(1, len(shares)):
            chosen = jnp.where(place == own, shares[own ^ position], chosen)
        ordered.append(chosen)
    return jnp.concatenate(ordered, axis=0)


def unpack_half(packed, which, offsets, channels, before=None):
    height = packed_rows(channels)
    rest = channels - LANES
    steps = round_up(offsets, 2) // 2 // UNPACK

    def kernel(which_ref, in_ref, *refs):
        out_ref = refs[-1]
        for position in range(UNPACK):
            value = in_ref[position * height : (position + 1) * height].astype(jnp.float32)
            out_ref[position, :, :LANES] = value[:channels]
            out_ref[position, : channels // 2, LANES:] = value[channels:, :rest]
            out_ref[position, channels // 2 :, LANES:] = value[channels:, rest:]

    extra = [] if before is None else [before]
    return pl.pallas_call(
        kernel,
        grid_spec=pltpu.PrefetchScalarGridSpec(
            num_scalar_prefetch=1,
            grid=(steps,),
            in_specs=[pl.BlockSpec((UNPACK * height, LANES), lambda k, which: (k, 0))]
            + [pl.BlockSpec(memory_space=pl.ANY)] * len(extra),
            out_specs=pl.BlockSpec(
                (UNPACK, channels, channels), lambda k, which: (which[0] * steps + k, 0, 0)
            ),
        ),
        out_shape=jax.ShapeDtypeStruct((offsets, channels, channels), jnp.float32),
        input_output_aliases={} if before is None else {2: 0},
        name="unpack_half",
    )(which.reshape(1).astype(jnp.int32), packed, *extra)


def forward_conv(features, weight, sources, targets, live, slots):
    rows, channels = features.shape
    offsets, _, pairs = sources.shape
    extended = round_up(rows + 8 * slots + 1, 8)
    ndir = len(live)

    def kernel(src_ref, dst_ref, x_ref, w_ref, summed_ref, kept_ref, *refs):
        out_refs = refs[:ndir]
        table, gbuf, vbuf, *sums = refs[ndir:]
        k = pl.program_id(0)

        @pl.when(k == 0)
        def _():
            fill_table(table, 0, x_ref[...])
            vbuf[...] = jnp.zeros_like(vbuf)
            for part in sums:
                part[: 2 * rows, :] = jnp.zeros((2 * rows, LANES), jnp.float32)
                for j in live:
                    part[pl.ds(2 * (rows + j * slots), 2 * slots), :] = jnp.zeros(
                        (2 * slots, LANES), jnp.float32
                    )

        gather_and_scatter(src_ref, table, gbuf, dst_ref, vbuf, sums, pairs)
        picked = joined(gbuf, pairs)
        kept_ref[0] = picked
        product = jnp.dot(picked[:, :channels], w_ref[0], preferred_element_type=jnp.float32)
        fill_table(vbuf, 0, product)

        @pl.when(k == offsets)
        def _():
            for first in range(0, rows, 256):
                summed_ref[pl.ds(first, 256), :] = chain_total(sums, first, 256, channels)
            for place, j in enumerate(live):
                out_refs[place][...] = chain_total(sums, rows + j * slots, slots, channels).astype(
                    jnp.bfloat16
                )

    now = lambda k: (jnp.minimum(k, offsets - 1), 0, 0)
    before = lambda k: (jnp.maximum(k - 1, 0), 0, 0)
    smem = lambda where: pl.BlockSpec((1, 1, pairs), where, memory_space=pltpu.SMEM)
    return pl.pallas_call(
        kernel,
        grid=(offsets + 1,),
        in_specs=[
            smem(now),
            smem(before),
            pl.BlockSpec((rows, channels), lambda k: (0, 0)),
            pl.BlockSpec((1, channels, channels), now),
        ],
        out_specs=[
            pl.BlockSpec((rows, channels), lambda k: (0, 0)),
            pl.BlockSpec((1, pairs, 2 * LANES), now),
        ]
        + [pl.BlockSpec((slots, channels), lambda k: (0, 0))] * ndir,
        out_shape=[
            jax.ShapeDtypeStruct((rows, channels), jnp.float32),
            jax.ShapeDtypeStruct((offsets, pairs, 2 * LANES), jnp.bfloat16),
        ]
        + [jax.ShapeDtypeStruct((slots, channels), jnp.bfloat16)] * ndir,
        scratch_shapes=[
            pltpu.VMEM((2 * rows, LANES), jnp.float32),
            pltpu.VMEM((2 * pairs, LANES), jnp.float32),
            pltpu.VMEM((2 * pairs, LANES), jnp.float32),
        ]
        + [pltpu.VMEM((2 * extended, LANES), jnp.float32)] * CHAINS,
        compiler_params=pltpu.CompilerParams(vmem_limit_bytes=VMEM_LIMIT),
        name="forward_conv",
    )(sources, targets, features, weight)


def landed_moments(summed, arrivals, places, count):
    rows, channels = summed.shape
    slots = arrivals[0].shape[0]
    total = slots * len(arrivals)

    def kernel(place_ref, count_ref, summed_ref, *refs):
        arrived = refs[: len(arrivals)]
        preact_ref, moments_ref, incoming = refs[len(arrivals) :]
        preact_ref[...] = summed_ref[...]
        for number, part in enumerate(arrived):
            incoming[number * slots : (number + 1) * slots, :] = part[...].astype(jnp.float32)

        @pl.loop(0, total, step=LAND_UNROLL)
        def _(start):
            for u in range(LAND_UNROLL):
                preact_ref[pl.ds(place_ref[start + u], 1), :] += incoming[pl.ds(start + u, 1), :]

        own = count_ref[0]
        own_float = own.astype(jnp.float32)
        block = 256

        def blocks(value):
            result = jnp.zeros((1, channels), jnp.float32)
            for first in range(0, rows, block):
                ids = first + lax.broadcasted_iota(jnp.int32, (block, 1), 0)
                part = value(preact_ref[first : first + block, :])
                result += jnp.sum(jnp.where(ids < own, part, 0.0), axis=0, keepdims=True)
            return result

        mean = blocks(lambda x: x) / own_float
        moments_ref[0:1, :] = jnp.full((1, channels), own_float)
        moments_ref[1:2, :] = mean
        moments_ref[2:3, :] = blocks(lambda x: (x - mean) * (x - mean))

    smem = pl.BlockSpec(memory_space=pltpu.SMEM)
    vmem = pl.BlockSpec(memory_space=pltpu.VMEM)
    return pl.pallas_call(
        kernel,
        in_specs=[smem, smem] + [vmem] * (1 + len(arrivals)),
        out_specs=[vmem, vmem],
        out_shape=[
            jax.ShapeDtypeStruct((rows, channels), jnp.float32),
            jax.ShapeDtypeStruct((3, channels), jnp.float32),
        ],
        scratch_shapes=[pltpu.VMEM((total, channels), jnp.float32)],
        compiler_params=pltpu.CompilerParams(vmem_limit_bytes=32 << 20),
        name="landed_moments",
    )(places, count, summed, *arrivals)


def backward_conv(pre_grad, returned, kept, weight, sources, targets, live, slots, done):
    rows, channels = pre_grad.shape
    offsets, _, pairs = sources.shape
    extended = round_up(rows + 8 * slots + 1, 8)
    ndir = len(live)
    height = packed_rows(channels)
    half = round_up(offsets, 2) // 2
    half_rows = round_up(half * height, HALF_ROWS)

    def kernel(src_ref, dst_ref, g_ref, x_ref, w_ref, *refs):
        ret_refs = refs[:ndir]
        wgrad_ref, xgrad_ref, rows_ref, table, gbuf, vbuf, *sums = refs[ndir:]
        k = pl.program_id(0)

        @pl.when(k == 0)
        def _():
            fill_table(table, 0, g_ref[...])
            for place, j in enumerate(live):
                fill_table(table, rows + j * slots, ret_refs[place][...])
            tail = 2 * (rows + 8 * slots)
            table[tail:, :] = jnp.zeros((2 * extended - tail, LANES), jnp.float32)
            vbuf[...] = jnp.zeros_like(vbuf)
            wgrad_ref[half * height : half_rows, :] = jnp.zeros(
                (half_rows - half * height, LANES), jnp.bfloat16
            )
            used = half_rows + (offsets - half) * height
            wgrad_ref[used:, :] = jnp.zeros((2 * half_rows - used, LANES), jnp.bfloat16)
            for part in sums:
                part[...] = jnp.zeros_like(part)

        def step(scatters, keeps):
            if scatters:
                gather_and_scatter(dst_ref, table, gbuf, src_ref, vbuf, sums, pairs)
            else:
                gather_rows(dst_ref, table, gbuf, pairs)
            whole = joined(gbuf, pairs)
            picked = whole[:, :channels]
            wgrad = lax.dot_general(
                x_ref[0, :, :channels],
                picked,
                (((0,), (0,)), ((), ())),
                preferred_element_type=jnp.float32,
            ).astype(jnp.bfloat16)
            first = jnp.where(k < half, k * height, half_rows + (k - half) * height)
            first = pl.multiple_of(first, 32)
            wgrad_ref[pl.ds(first, channels), :] = wgrad[:, :LANES]
            wgrad_ref[pl.ds(first + channels, channels // 2), :] = jnp.concatenate(
                [wgrad[: channels // 2, LANES:], wgrad[channels // 2 :, LANES:]], axis=1
            )
            if keeps:
                rows_ref[0] = whole
            else:
                product = lax.dot_general(
                    picked, w_ref[0], (((1,), (1,)), ((), ())), preferred_element_type=jnp.float32
                )
                fill_table(vbuf, 0, product)

        pl.when(k < done)(lambda: step(True, False))
        pl.when(k == done)(lambda: step(True, True))
        pl.when(k > done)(lambda: step(False, True))

        @pl.when(k == offsets - 1)
        def _():
            for first in range(0, rows, 256):
                xgrad_ref[pl.ds(first, 256), :] = chain_total(sums, first, 256, channels)

    now = lambda k: (jnp.minimum(k, offsets - 1), 0, 0)
    before = lambda k: (jnp.clip(k - 1, 0, done - 1), 0, 0)
    later = lambda k: (jnp.maximum(k - done, 0), 0, 0)
    early = lambda k: (jnp.minimum(k, done - 1), 0, 0)
    smem = lambda where: pl.BlockSpec((1, 1, pairs), where, memory_space=pltpu.SMEM)
    return pl.pallas_call(
        kernel,
        grid=(offsets,),
        in_specs=[
            smem(before),
            smem(now),
            pl.BlockSpec((rows, channels), lambda k: (0, 0)),
            pl.BlockSpec((1, pairs, 2 * LANES), now),
            pl.BlockSpec((1, channels, channels), early),
        ]
        + [pl.BlockSpec((slots, channels), lambda k: (0, 0))] * ndir,
        out_specs=[
            pl.BlockSpec((2 * half_rows, LANES), lambda k: (0, 0)),
            pl.BlockSpec((rows, channels), lambda k: (0, 0)),
            pl.BlockSpec((1, pairs, 2 * LANES), later),
        ],
        out_shape=[
            jax.ShapeDtypeStruct((2 * half_rows, LANES), jnp.bfloat16),
            jax.ShapeDtypeStruct((rows, channels), jnp.float32),
            jax.ShapeDtypeStruct((offsets - done, pairs, 2 * LANES), jnp.bfloat16),
        ],
        scratch_shapes=[
            pltpu.VMEM((2 * extended, LANES), jnp.float32),
            pltpu.VMEM((2 * pairs, LANES), jnp.float32),
            pltpu.VMEM((2 * pairs, LANES), jnp.float32),
        ]
        + [pltpu.VMEM((2 * rows, LANES), jnp.float32)] * CHAINS,
        compiler_params=pltpu.CompilerParams(vmem_limit_bytes=VMEM_LIMIT),
        name="backward_conv",
    )(sources, targets, pre_grad, kept, weight, *returned)


def input_grads(grad_rows, weight, sources, first, last, previous, rows, base):
    pairs = grad_rows.shape[1]
    offsets, channels, _ = weight.shape
    count = last - first
    final = last == offsets

    def kernel(src_ref, g_ref, w_ref, *rest):
        refs = list(rest)
        before = refs.pop(0) if previous is not None else None
        xgrad_ref, vbuf, sums = refs[0], refs[1], refs[2:]
        k = pl.program_id(0)

        @pl.when(k == 0)
        def _():
            vbuf[...] = jnp.zeros_like(vbuf)
            for part in sums[1 if previous is not None else 0 :]:
                part[...] = jnp.zeros_like(part)
            if previous is not None:
                fill_table(sums[0], 0, before[...])

        product = lax.dot_general(
            g_ref[0, :, :channels], w_ref[0], (((1,), (1,)), ((), ())), preferred_element_type=jnp.float32
        )
        fill_table(vbuf, 0, product)
        scatter_rows(src_ref, vbuf, sums, pairs)

        @pl.when(k == count - 1)
        def _():
            for start in range(0, rows, 256):
                xgrad_ref[pl.ds(start, 256), :] = chain_total(sums, start, 256, channels).astype(
                    xgrad_ref.dtype
                )

    each = lambda k: (k + first, 0, 0)
    whole = pl.BlockSpec((rows, channels), lambda k: (0, 0))
    return pl.pallas_call(
        kernel,
        grid=(count,),
        in_specs=[
            pl.BlockSpec((1, 1, pairs), each, memory_space=pltpu.SMEM),
            pl.BlockSpec((1, pairs, 2 * LANES), lambda k: (k + first - base, 0, 0)),
            pl.BlockSpec((1, channels, channels), each),
        ]
        + ([whole] if previous is not None else []),
        out_specs=whole,
        out_shape=jax.ShapeDtypeStruct((rows, channels), jnp.bfloat16 if final else jnp.float32),
        scratch_shapes=[pltpu.VMEM((2 * pairs, LANES), jnp.float32)]
        + [pltpu.VMEM((2 * rows, LANES), jnp.float32)] * CHAINS,
        compiler_params=pltpu.CompilerParams(vmem_limit_bytes=VMEM_LIMIT),
        cost_estimate=pl.CostEstimate(
            flops=count * COST_FLOPS, bytes_accessed=2 * count * pairs * channels, transcendentals=0
        ),
        name="input_grads",
    )(sources, grad_rows, weight, *([previous] if previous is not None else []))


def covered(grad_rows, weight, sources, previous, sent, done, count, rows, base):
    offsets = weight.shape[0]
    last = min(offsets, done + count)
    grad_rows, sent = lax.optimization_barrier((grad_rows, sent))
    return input_grads(grad_rows, weight, sources, done, last, previous, rows, base), sent, last


def on_device(
    features, weight, norm_gain, norm_shift, cotangent, counts, in_rows, out_slots, land_rows
):
    regions = lax.axis_size("region")
    live = live_directions(regions)
    voxels = features[0]
    row_count, channels = voxels.shape
    sources = (in_rows[0, 0] * 2)[:, None, :]
    targets = (out_slots[0, 0] * 2)[:, None, :]
    slot_count = land_rows.shape[3]
    places = jnp.concatenate([land_rows[0, 0, j] for j in live])
    summed, kept, *outgoing = forward_conv(voxels, weight, sources, targets, live, slot_count)
    arrivals = [
        lax.ppermute(outgoing[place], "region", neighbour_pairs(regions, DIRECTIONS[j]))
        for place, j in enumerate(live)
    ]
    preact, moments = landed_moments(summed, arrivals, places, counts[0])
    alive = (lax.broadcasted_iota(jnp.int32, (row_count, 1), 0) < counts[0, 0]).astype(jnp.float32)
    count_total, average, square = all_moments(moments)
    variance = square / count_total
    inverse = lax.rsqrt(variance + EPSILON)
    normed = (preact - average) * inverse
    shifted = norm_gain * normed + norm_shift
    sigma = jax.nn.sigmoid(shifted)
    slope = sigma * (1.0 + shifted * (1.0 - sigma)) * alive
    activated = (shifted * sigma * alive).astype(jnp.bfloat16)
    upstream = cotangent[0].astype(jnp.float32) * slope
    gain_grad, shift_grad = all_sum(
        jnp.stack([jnp.sum(upstream * normed, axis=0), jnp.sum(upstream, axis=0)])
    )
    pre_grad = (
        norm_gain
        * inverse
        * (upstream - shift_grad / count_total - normed * gain_grad / count_total)
        * alive
    ).astype(jnp.bfloat16)
    picked = pre_grad[places].reshape(len(live), slot_count, channels)
    returned = [
        lax.ppermute(
            picked[place], "region", [(b, a) for a, b in neighbour_pairs(regions, DIRECTIONS[j])]
        )
        for place, j in enumerate(live)
    ]
    offsets = weight.shape[0]
    base = offsets - sum(COVER_SUM.values()) - sum(COVER_SHARE.values())
    done = base
    total, input_grad, grad_rows = backward_conv(
        pre_grad, returned, kept, weight, sources, targets, live, slot_count, base
    )
    rounds = reduction_rounds()
    for number, group in enumerate(rounds):
        sent = sent_shares(total, group)
        if number in COVER_SUM:
            input_grad, sent, done = covered(
                grad_rows, weight, sources, input_grad, sent, done, COVER_SUM[number], row_count, base
            )
        total = sum_share(total, sent, group)
        if number in COVER_SUM:
            total, input_grad = lax.optimization_barrier((total, input_grad))
    own = total.astype(jnp.bfloat16)
    for number in range(len(rounds) - 1, 0, -1):
        sent = own
        if number in COVER_SHARE:
            input_grad, sent, done = covered(
                grad_rows, weight, sources, input_grad, sent, done, COVER_SHARE[number], row_count, base
            )
        own = gathered_shares(sent, rounds[number])
        if number in COVER_SHARE:
            own, input_grad = lax.optimization_barrier((own, input_grad))
    place, ((_, permutation),) = place_in(rounds[0])
    other = lax.ppermute(own, ("region", "dp"), permutation)
    weight_grad = unpack_half(own, place, weight.shape[0], channels)
    weight_grad = unpack_half(other, 1 - place, weight.shape[0], channels, weight_grad)
    return (activated[None], input_grad[None], weight_grad, gain_grad, shift_grad)


def solution(mesh):
    return jax.shard_map(
        on_device,
        mesh=mesh,
        in_specs=(
            P("dp", "region", None),
            P(),
            P(),
            P(),
            P("dp", "region", None),
            P("dp", "region"),
            P("dp", "region", None, None),
            P("dp", "region", None, None),
            P("dp", "region", None, None),
        ),
        out_specs=(P("dp", "region", None), P("dp", "region", None), P(), P(), P()),
        check_vma=False,
    )
```

```python
import jax
import jax.numpy as jnp
from jax import lax
from jax.experimental import pallas as pl
from jax.experimental.pallas import tpu as pltpu
from jax.sharding import PartitionSpec as P

GRID_W = 8
DIRECTIONS = ((-1, -1), (-1, 0), (-1, 1), (0, -1), (0, 1), (1, -1), (1, 0), (1, 1))
EPSILON = 1e-05
LANES = 128
CHAINS = 8
SCATTER_UNROLL = 32
HALF_ROWS = 4096
LAND_UNROLL = 16
GATHER_UNROLL = 256
COVER_SUM = {1: 4}
COVER_SHARE = {1: 4}
COST_FLOPS = 2 << 30
UNPACK = 7
VMEM_LIMIT = 60 << 20


def live_directions(regions):
    rows = regions // GRID_W
    return [j for j, (dr, dc) in enumerate(DIRECTIONS) if abs(dr) < rows and abs(dc) < GRID_W]


def neighbour_pairs(regions, step):
    rows = regions // GRID_W
    pairs = []
    for r in range(regions):
        row, col = r // GRID_W + step[0], r % GRID_W + step[1]
        if 0 <= row < rows and 0 <= col < GRID_W:
            pairs.append((r, row * GRID_W + col))
    return pairs


def fill_table(table, first, rows):
    count, channels = rows.shape
    rows = rows.astype(jnp.float32)
    table[pl.ds(2 * first, count, stride=2), :] = rows[:, :LANES]
    rest = jnp.concatenate(
        [rows[:, LANES:], jnp.zeros((count, 2 * LANES - channels), jnp.float32)], axis=1
    )
    table[pl.ds(2 * first + 1, count, stride=2), :] = rest


def gather_rows(index, table, buffer, pairs):
    @pl.loop(0, pairs, step=GATHER_UNROLL)
    def _(start):
        for u in range(GATHER_UNROLL):
            source = pl.multiple_of(index[0, 0, start + u], 2)
            target = pl.multiple_of((start + u) * 2, 2)
            buffer[pl.ds(target, 2), :] = table[pl.ds(source, 2), :]


def scatter_rows(index, buffer, sums, pairs):
    per_chain = pairs // CHAINS

    @pl.loop(0, per_chain, step=SCATTER_UNROLL)
    def _(start):
        for u in range(SCATTER_UNROLL):
            for chain in range(CHAINS):
                pair = chain * per_chain + start + u
                target = pl.multiple_of(index[0, 0, pair], 2)
                source = pl.multiple_of(pair * 2, 2)
                sums[chain][pl.ds(target, 2), :] += buffer[pl.ds(source, 2), :]


def gather_and_scatter(gather_index, table, gbuf, scatter_index, vbuf, sums, pairs):
    per_chain = pairs // CHAINS

    @pl.loop(0, per_chain, step=SCATTER_UNROLL)
    def _(start):
        for u in range(SCATTER_UNROLL):
            for chain in range(CHAINS):
                pair = chain * per_chain + start + u
                place = pl.multiple_of(pair * 2, 2)
                target = pl.multiple_of(scatter_index[0, 0, pair], 2)
                sums[chain][pl.ds(target, 2), :] += vbuf[pl.ds(place, 2), :]
                source = pl.multiple_of(gather_index[0, 0, pair], 2)
                gbuf[pl.ds(place, 2), :] = table[pl.ds(source, 2), :]


def joined(buffer, pairs):
    low = buffer[pl.ds(0, pairs, stride=2), :].astype(jnp.bfloat16)
    high = buffer[pl.ds(1, pairs, stride=2), :].astype(jnp.bfloat16)
    return jnp.concatenate([low, high], axis=1)


def chain_total(sums, first, count, channels):
    low = sums[0][pl.ds(2 * first, count, stride=2), :]
    high = sums[0][pl.ds(2 * first + 1, count, stride=2), :]
    for part in sums[1:]:
        low += part[pl.ds(2 * first, count, stride=2), :]
        high += part[pl.ds(2 * first + 1, count, stride=2), :]
    return jnp.concatenate([low, high[:, : channels - LANES]], axis=1)


def round_up(n, m):
    return (n + m - 1) // m * m


def packed_rows(channels):
    return channels + channels // 2


def doubling_steps():
    steps = []
    for axis in ("dp", "region"):
        stride = 1
        while stride < lax.axis_size(axis):
            steps.append((stride, axis))
            stride *= 2
    return [(axis, stride) for stride, axis in sorted(steps)]


def exchange(value, axis, stride):
    return lax.ppermute(value, axis, [(i, i ^ stride) for i in range(lax.axis_size(axis))])


def from_all(value):
    count = lax.axis_size("region") * lax.axis_size("dp")
    flat = jnp.broadcast_to(value.reshape(1, 1, -1), (count, 1, value.size))
    flat = lax.all_to_all(flat, ("region", "dp"), 0, 0, tiled=True)
    return flat.reshape((count,) + value.shape)


def all_sum(value):
    return jnp.sum(from_all(value), axis=0)


def all_moments(value):
    value = from_all(value)
    count, mean, square = value[:, 0], value[:, 1], value[:, 2]
    total = jnp.sum(count, axis=0)
    average = jnp.sum(count * mean, axis=0) / total
    gap = mean - average
    return total, average, jnp.sum(square + count * gap * gap, axis=0)


def reduction_rounds():
    steps = doubling_steps()
    return [steps[:1]] + [steps[i : i + 2] for i in range(1, len(steps), 2)]


def place_in(group):
    place = 0
    for bit, (axis, stride) in enumerate(group):
        place = place + (lax.axis_index(axis) // stride) % 2 * (1 << bit)
    inner = lax.axis_size("dp")
    count = inner * lax.axis_size("region")
    permutations = []
    for mask in range(1, 1 << len(group)):
        flip = 0
        for bit, (axis, stride) in enumerate(group):
            if mask >> bit & 1:
                flip ^= stride * (inner if axis == "region" else 1)
        permutations.append((mask, [(i, i ^ flip) for i in range(count)]))
    return place, permutations


def sent_shares(value, group):
    place, permutations = place_in(group)
    share = value.shape[0] >> len(group)
    return [
        lax.dynamic_slice_in_dim(value, (place ^ mask) * share, share, 0).astype(jnp.bfloat16)
        for mask, _ in permutations
    ]


def sum_share(value, sent, group):
    place, permutations = place_in(group)
    share = value.shape[0] >> len(group)
    total = lax.dynamic_slice_in_dim(value, place * share, share, 0).astype(jnp.float32)
    for part, (_, permutation) in zip(sent, permutations):
        got = lax.ppermute(part, ("region", "dp"), permutation)
        total = total + got.astype(jnp.float32)
    return total


def gathered_shares(value, group):
    place, permutations = place_in(group)
    shares = [value] + [
        lax.ppermute(value, ("region", "dp"), permutation) for _, permutation in permutations
    ]
    ordered = []
    for position in range(len(shares)):
        chosen = shares[position]
        for own in range(1, len(shares)):
            chosen = jnp.where(place == own, shares[own ^ position], chosen)
        ordered.append(chosen)
    return jnp.concatenate(ordered, axis=0)


def unpack_half(packed, which, offsets, channels, before=None):
    height = packed_rows(channels)
    rest = channels - LANES
    steps = round_up(offsets, 2) // 2 // UNPACK

    def kernel(which_ref, in_ref, *refs):
        out_ref = refs[-1]
        for position in range(UNPACK):
            value = in_ref[position * height : (position + 1) * height].astype(jnp.float32)
            out_ref[position, :, :LANES] = value[:channels]
            out_ref[position, : channels // 2, LANES:] = value[channels:, :rest]
            out_ref[position, channels // 2 :, LANES:] = value[channels:, rest:]

    extra = [] if before is None else [before]
    return pl.pallas_call(
        kernel,
        grid_spec=pltpu.PrefetchScalarGridSpec(
            num_scalar_prefetch=1,
            grid=(steps,),
            in_specs=[pl.BlockSpec((UNPACK * height, LANES), lambda k, which: (k, 0))]
            + [pl.BlockSpec(memory_space=pl.ANY)] * len(extra),
            out_specs=pl.BlockSpec(
                (UNPACK, channels, channels), lambda k, which: (which[0] * steps + k, 0, 0)
            ),
        ),
        out_shape=jax.ShapeDtypeStruct((offsets, channels, channels), jnp.float32),
        input_output_aliases={} if before is None else {2: 0},
        name="unpack_half",
    )(which.reshape(1).astype(jnp.int32), packed, *extra)


def forward_conv(features, weight, sources, targets, live, slots):
    rows, channels = features.shape
    offsets, _, pairs = sources.shape
    extended = round_up(rows + 8 * slots + 1, 8)
    ndir = len(live)

    def kernel(src_ref, dst_ref, x_ref, w_ref, summed_ref, kept_ref, *refs):
        out_refs = refs[:ndir]
        table, gbuf, vbuf, *sums = refs[ndir:]
        k = pl.program_id(0)

        @pl.when(k == 0)
        def _():
            fill_table(table, 0, x_ref[...])
            vbuf[...] = jnp.zeros_like(vbuf)
            for part in sums:
                part[: 2 * rows, :] = jnp.zeros((2 * rows, LANES), jnp.float32)
                for j in live:
                    part[pl.ds(2 * (rows + j * slots), 2 * slots), :] = jnp.zeros(
                        (2 * slots, LANES), jnp.float32
                    )

        gather_and_scatter(src_ref, table, gbuf, dst_ref, vbuf, sums, pairs)
        picked = joined(gbuf, pairs)
        kept_ref[0] = picked
        product = jnp.dot(picked[:, :channels], w_ref[0], preferred_element_type=jnp.float32)
        fill_table(vbuf, 0, product)

        @pl.when(k == offsets)
        def _():
            for first in range(0, rows, 256):
                summed_ref[pl.ds(first, 256), :] = chain_total(sums, first, 256, channels)
            for place, j in enumerate(live):
                out_refs[place][...] = chain_total(sums, rows + j * slots, slots, channels).astype(
                    jnp.bfloat16
                )

    now = lambda k: (jnp.minimum(k, offsets - 1), 0, 0)
    before = lambda k: (jnp.maximum(k - 1, 0), 0, 0)
    smem = lambda where: pl.BlockSpec((1, 1, pairs), where, memory_space=pltpu.SMEM)
    return pl.pallas_call(
        kernel,
        grid=(offsets + 1,),
        in_specs=[
            smem(now),
            smem(before),
            pl.BlockSpec((rows, channels), lambda k: (0, 0)),
            pl.BlockSpec((1, channels, channels), now),
        ],
        out_specs=[
            pl.BlockSpec((rows, channels), lambda k: (0, 0)),
            pl.BlockSpec((1, pairs, 2 * LANES), now),
        ]
        + [pl.BlockSpec((slots, channels), lambda k: (0, 0))] * ndir,
        out_shape=[
            jax.ShapeDtypeStruct((rows, channels), jnp.float32),
            jax.ShapeDtypeStruct((offsets, pairs, 2 * LANES), jnp.bfloat16),
        ]
        + [jax.ShapeDtypeStruct((slots, channels), jnp.bfloat16)] * ndir,
        scratch_shapes=[
            pltpu.VMEM((2 * rows, LANES), jnp.float32),
            pltpu.VMEM((2 * pairs, LANES), jnp.float32),
            pltpu.VMEM((2 * pairs, LANES), jnp.float32),
        ]
        + [pltpu.VMEM((2 * extended, LANES), jnp.float32)] * CHAINS,
        compiler_params=pltpu.CompilerParams(vmem_limit_bytes=VMEM_LIMIT),
        name="forward_conv",
    )(sources, targets, features, weight)


def landed_moments(summed, arrivals, places, count):
    rows, channels = summed.shape
    slots = arrivals[0].shape[0]
    total = slots * len(arrivals)

    def kernel(place_ref, count_ref, summed_ref, *refs):
        arrived = refs[: len(arrivals)]
        preact_ref, moments_ref, incoming = refs[len(arrivals) :]
        preact_ref[...] = summed_ref[...]
        for number, part in enumerate(arrived):
            incoming[number * slots : (number + 1) * slots, :] = part[...].astype(jnp.float32)

        @pl.loop(0, total, step=LAND_UNROLL)
        def _(start):
            for u in range(LAND_UNROLL):
                preact_ref[pl.ds(place_ref[start + u], 1), :] += incoming[pl.ds(start + u, 1), :]

        own = count_ref[0]
        own_float = own.astype(jnp.float32)
        block = 256

        def blocks(value):
            result = jnp.zeros((1, channels), jnp.float32)
            for first in range(0, rows, block):
                ids = first + lax.broadcasted_iota(jnp.int32, (block, 1), 0)
                part = value(preact_ref[first : first + block, :])
                result += jnp.sum(jnp.where(ids < own, part, 0.0), axis=0, keepdims=True)
            return result

        mean = blocks(lambda x: x) / own_float
        moments_ref[0:1, :] = jnp.full((1, channels), own_float)
        moments_ref[1:2, :] = mean
        moments_ref[2:3, :] = blocks(lambda x: (x - mean) * (x - mean))

    smem = pl.BlockSpec(memory_space=pltpu.SMEM)
    vmem = pl.BlockSpec(memory_space=pltpu.VMEM)
    return pl.pallas_call(
        kernel,
        in_specs=[smem, smem] + [vmem] * (1 + len(arrivals)),
        out_specs=[vmem, vmem],
        out_shape=[
            jax.ShapeDtypeStruct((rows, channels), jnp.float32),
            jax.ShapeDtypeStruct((3, channels), jnp.float32),
        ],
        scratch_shapes=[pltpu.VMEM((total, channels), jnp.float32)],
        compiler_params=pltpu.CompilerParams(vmem_limit_bytes=32 << 20),
        name="landed_moments",
    )(places, count, summed, *arrivals)


def backward_conv(pre_grad, returned, kept, weight, sources, targets, live, slots, done):
    rows, channels = pre_grad.shape
    offsets, _, pairs = sources.shape
    extended = round_up(rows + 8 * slots + 1, 8)
    ndir = len(live)
    height = packed_rows(channels)
    half = round_up(offsets, 2) // 2
    half_rows = round_up(half * height, HALF_ROWS)

    def kernel(src_ref, dst_ref, g_ref, x_ref, w_ref, *refs):
        ret_refs = refs[:ndir]
        wgrad_ref, xgrad_ref, rows_ref, table, gbuf, vbuf, *sums = refs[ndir:]
        k = pl.program_id(0)

        @pl.when(k == 0)
        def _():
            fill_table(table, 0, g_ref[...])
            for place, j in enumerate(live):
                fill_table(table, rows + j * slots, ret_refs[place][...])
            tail = 2 * (rows + 8 * slots)
            table[tail:, :] = jnp.zeros((2 * extended - tail, LANES), jnp.float32)
            vbuf[...] = jnp.zeros_like(vbuf)
            wgrad_ref[half * height : half_rows, :] = jnp.zeros(
                (half_rows - half * height, LANES), jnp.bfloat16
            )
            used = half_rows + (offsets - half) * height
            wgrad_ref[used:, :] = jnp.zeros((2 * half_rows - used, LANES), jnp.bfloat16)
            for part in sums:
                part[...] = jnp.zeros_like(part)

        def step(scatters, keeps):
            if scatters:
                gather_and_scatter(dst_ref, table, gbuf, src_ref, vbuf, sums, pairs)
            else:
                gather_rows(dst_ref, table, gbuf, pairs)
            whole = joined(gbuf, pairs)
            picked = whole[:, :channels]
            wgrad = lax.dot_general(
                x_ref[0, :, :channels],
                picked,
                (((0,), (0,)), ((), ())),
                preferred_element_type=jnp.float32,
            ).astype(jnp.bfloat16)
            first = jnp.where(k < half, k * height, half_rows + (k - half) * height)
            first = pl.multiple_of(first, 32)
            wgrad_ref[pl.ds(first, channels), :] = wgrad[:, :LANES]
            wgrad_ref[pl.ds(first + channels, channels // 2), :] = jnp.concatenate(
                [wgrad[: channels // 2, LANES:], wgrad[channels // 2 :, LANES:]], axis=1
            )
            if keeps:
                rows_ref[0] = whole
            else:
                product = lax.dot_general(
                    picked, w_ref[0], (((1,), (1,)), ((), ())), preferred_element_type=jnp.float32
                )
                fill_table(vbuf, 0, product)

        pl.when(k < done)(lambda: step(True, False))
        pl.when(k == done)(lambda: step(True, True))
        pl.when(k > done)(lambda: step(False, True))

        @pl.when(k == offsets - 1)
        def _():
            for first in range(0, rows, 256):
                xgrad_ref[pl.ds(first, 256), :] = chain_total(sums, first, 256, channels)

    now = lambda k: (jnp.minimum(k, offsets - 1), 0, 0)
    before = lambda k: (jnp.clip(k - 1, 0, done - 1), 0, 0)
    later = lambda k: (jnp.maximum(k - done, 0), 0, 0)
    early = lambda k: (jnp.minimum(k, done - 1), 0, 0)
    smem = lambda where: pl.BlockSpec((1, 1, pairs), where, memory_space=pltpu.SMEM)
    return pl.pallas_call(
        kernel,
        grid=(offsets,),
        in_specs=[
            smem(before),
            smem(now),
            pl.BlockSpec((rows, channels), lambda k: (0, 0)),
            pl.BlockSpec((1, pairs, 2 * LANES), now),
            pl.BlockSpec((1, channels, channels), early),
        ]
        + [pl.BlockSpec((slots, channels), lambda k: (0, 0))] * ndir,
        out_specs=[
            pl.BlockSpec((2 * half_rows, LANES), lambda k: (0, 0)),
            pl.BlockSpec((rows, channels), lambda k: (0, 0)),
            pl.BlockSpec((1, pairs, 2 * LANES), later),
        ],
        out_shape=[
            jax.ShapeDtypeStruct((2 * half_rows, LANES), jnp.bfloat16),
            jax.ShapeDtypeStruct((rows, channels), jnp.float32),
            jax.ShapeDtypeStruct((offsets - done, pairs, 2 * LANES), jnp.bfloat16),
        ],
        scratch_shapes=[
            pltpu.VMEM((2 * extended, LANES), jnp.float32),
            pltpu.VMEM((2 * pairs, LANES), jnp.float32),
            pltpu.VMEM((2 * pairs, LANES), jnp.float32),
        ]
        + [pltpu.VMEM((2 * rows, LANES), jnp.float32)] * CHAINS,
        compiler_params=pltpu.CompilerParams(vmem_limit_bytes=VMEM_LIMIT),
        name="backward_conv",
    )(sources, targets, pre_grad, kept, weight, *returned)


def input_grads(grad_rows, weight, sources, first, last, previous, rows, base):
    pairs = grad_rows.shape[1]
    offsets, channels, _ = weight.shape
    count = last - first
    final = last == offsets

    def kernel(src_ref, g_ref, w_ref, *rest):
        refs = list(rest)
        before = refs.pop(0) if previous is not None else None
        xgrad_ref, vbuf, sums = refs[0], refs[1], refs[2:]
        k = pl.program_id(0)

        @pl.when(k == 0)
        def _():
            vbuf[...] = jnp.zeros_like(vbuf)
            for part in sums[1 if previous is not None else 0 :]:
                part[...] = jnp.zeros_like(part)
            if previous is not None:
                fill_table(sums[0], 0, before[...])

        product = lax.dot_general(
            g_ref[0, :, :channels], w_ref[0], (((1,), (1,)), ((), ())), preferred_element_type=jnp.float32
        )
        fill_table(vbuf, 0, product)
        scatter_rows(src_ref, vbuf, sums, pairs)

        @pl.when(k == count - 1)
        def _():
            for start in range(0, rows, 256):
                xgrad_ref[pl.ds(start, 256), :] = chain_total(sums, start, 256, channels).astype(
                    xgrad_ref.dtype
                )

    each = lambda k: (k + first, 0, 0)
    whole = pl.BlockSpec((rows, channels), lambda k: (0, 0))
    return pl.pallas_call(
        kernel,
        grid=(count,),
        in_specs=[
            pl.BlockSpec((1, 1, pairs), each, memory_space=pltpu.SMEM),
            pl.BlockSpec((1, pairs, 2 * LANES), lambda k: (k + first - base, 0, 0)),
            pl.BlockSpec((1, channels, channels), each),
        ]
        + ([whole] if previous is not None else []),
        out_specs=whole,
        out_shape=jax.ShapeDtypeStruct((rows, channels), jnp.bfloat16 if final else jnp.float32),
        scratch_shapes=[pltpu.VMEM((2 * pairs, LANES), jnp.float32)]
        + [pltpu.VMEM((2 * rows, LANES), jnp.float32)] * CHAINS,
        compiler_params=pltpu.CompilerParams(vmem_limit_bytes=VMEM_LIMIT),
        cost_estimate=pl.CostEstimate(
            flops=count * COST_FLOPS, bytes_accessed=2 * count * pairs * channels, transcendentals=0
        ),
        name="input_grads",
    )(sources, grad_rows, weight, *([previous] if previous is not None else []))


def covered(grad_rows, weight, sources, previous, sent, done, count, rows, base):
    offsets = weight.shape[0]
    last = min(offsets, done + count)
    grad_rows, sent = lax.optimization_barrier((grad_rows, sent))
    return input_grads(grad_rows, weight, sources, done, last, previous, rows, base), sent, last


def on_device(
    features, weight, norm_gain, norm_shift, cotangent, counts, in_rows, out_slots, land_rows
):
    regions = lax.axis_size("region")
    live = live_directions(regions)
    voxels = features[0]
    row_count, channels = voxels.shape
    sources = (in_rows[0, 0] * 2)[:, None, :]
    targets = (out_slots[0, 0] * 2)[:, None, :]
    slot_count = land_rows.shape[3]
    places = jnp.concatenate([land_rows[0, 0, j] for j in live])
    summed, kept, *outgoing = forward_conv(voxels, weight, sources, targets, live, slot_count)
    arrivals = [
        lax.ppermute(outgoing[place], "region", neighbour_pairs(regions, DIRECTIONS[j]))
        for place, j in enumerate(live)
    ]
    preact, moments = landed_moments(summed, arrivals, places, counts[0])
    alive = (lax.broadcasted_iota(jnp.int32, (row_count, 1), 0) < counts[0, 0]).astype(jnp.float32)
    count_total, average, square = all_moments(moments)
    variance = square / count_total
    inverse = lax.rsqrt(variance + EPSILON)
    normed = (preact - average) * inverse
    shifted = norm_gain * normed + norm_shift
    sigma = jax.nn.sigmoid(shifted)
    slope = sigma * (1.0 + shifted * (1.0 - sigma)) * alive
    activated = (shifted * sigma * alive).astype(jnp.bfloat16)
    upstream = cotangent[0].astype(jnp.float32) * slope
    gain_grad, shift_grad = all_sum(
        jnp.stack([jnp.sum(upstream * normed, axis=0), jnp.sum(upstream, axis=0)])
    )
    pre_grad = (
        norm_gain
        * inverse
        * (upstream - shift_grad / count_total - normed * gain_grad / count_total)
        * alive
    ).astype(jnp.bfloat16)
    picked = pre_grad[places].reshape(len(live), slot_count, channels)
    returned = [
        lax.ppermute(
            picked[place], "region", [(b, a) for a, b in neighbour_pairs(regions, DIRECTIONS[j])]
        )
        for place, j in enumerate(live)
    ]
    offsets = weight.shape[0]
    base = offsets - sum(COVER_SUM.values()) - sum(COVER_SHARE.values())
    done = base
    total, input_grad, grad_rows = backward_conv(
        pre_grad, returned, kept, weight, sources, targets, live, slot_count, base
    )
    rounds = reduction_rounds()
    for number, group in enumerate(rounds):
        sent = sent_shares(total, group)
        if number in COVER_SUM:
            input_grad, sent, done = covered(
                grad_rows, weight, sources, input_grad, sent, done, COVER_SUM[number], row_count, base
            )
        total = sum_share(total, sent, group)
        if number in COVER_SUM:
            total, input_grad = lax.optimization_barrier((total, input_grad))
    own = total.astype(jnp.bfloat16)
    for number in range(len(rounds) - 1, 0, -1):
        sent = own
        if number in COVER_SHARE:
            input_grad, sent, done = covered(
                grad_rows, weight, sources, input_grad, sent, done, COVER_SHARE[number], row_count, base
            )
        own = gathered_shares(sent, rounds[number])
        if number in COVER_SHARE:
            own, input_grad = lax.optimization_barrier((own, input_grad))
    place, ((_, permutation),) = place_in(rounds[0])
    other = lax.ppermute(own, ("region", "dp"), permutation)
    weight_grad = unpack_half(own, place, weight.shape[0], channels)
    weight_grad = unpack_half(other, 1 - place, weight.shape[0], channels, weight_grad)
    return (activated[None], input_grad[None], weight_grad, gain_grad, shift_grad)


def solution(mesh):
    return jax.shard_map(
        on_device,
        mesh=mesh,
        in_specs=(
            P("dp", "region", None),
            P(),
            P(),
            P(),
            P("dp", "region", None),
            P("dp", "region"),
            P("dp", "region", None, None),
            P("dp", "region", None, None),
            P("dp", "region", None, None),
        ),
        out_specs=(P("dp", "region", None), P("dp", "region", None), P(), P(), P()),
        check_vma=False,
    )
```
